32 devices in a mesh: seq: 4 (over x, core), chan: 8 (over z, y).
Axes of the slice: x: 2, y: 2, z: 4, core: 2. Of those that a mesh axis runs over, the one named last changes fastest.
Arguments:
- frames_in: bfloat16 [8192, 4096], P('seq', 'chan'), may hold values from -6 to 6
- gate_in: bfloat16 [8192, 4096], P('seq', 'chan'), may hold values from -6 to 6
- in_keys: bfloat16 [8192, 128], P('seq'), may hold values from -6 to 6
- out_keys: bfloat16 [8192, 128], P('seq'), may hold values from -6 to 6
- step_size: float32 [8192, 64], P('seq', 'chan'), may hold values from 0 to 1.6
- decay_rate: float32 [64], P('chan'), may hold values from 0.5 to 2
- skip_gain: float32 [64], P('chan'), may hold values from 0.5 to 2
- out_weight: bfloat16 [4096, 2048], P('chan'), may hold values from -0.09375 to 0.09375
- codebook: bfloat16 [65536, 512], P('chan'), may hold values from -6 to 6
- code_index: int32 [8192, 4], P(('seq', 'chan')), may hold values from 0 to 65535, as said below
- upstream: bfloat16 [8192, 2048], P(('seq', 'chan')), may hold values from -6 to 6
Outputs:
- latent: bfloat16 [8192, 2048], P(('seq', 'chan'))
- latent_grad: float32 [8192, 2048], P(('seq', 'chan'))
- codebook_grad: float32 [65536, 512], P('chan')
The draws below stay inside these ranges and needn't reach their ends.
Inputs may be any that keep to these rules, and one draw needn't show every extreme that they name: `code_index`: the codebook's entries fall into 8 shards of 65536 / 8 consecutive entries. Among the codes of the frames of one device (one index of seq+chan, 4 codes a frame), each shard is named at most 128 times and at least 128 - 1 times.
All inputs are finite; a program needn't handle non-finite values.
Results may differ from the reference program's by a relative error of at most 0.009.
Values may be sent and summed in bfloat16 or wider, within the bound.
No kernel may reach another device: no remote copies, remote signals or barrier semaphores. Data moves between devices by JAX's collectives and lax.ppermute only.
A program may use at most 128 MiB of HBM per device.

```python
import math
import jax
import jax.numpy as jnp
from jax import lax

D = 2048
HEADS = 64
HEAD_DIM = 64
STATE = 128
CODES = 65536
GROUPS = 4
BLOCK = 256
FRAMES_DEV = 2048
INNER = 4096
CODE_DIM = 512
SAMPLES_OVERALL = 8192
N_SEQ = 4
N_CHAN = 8


def rates_and_steps(key):
    inner_key = jax.random.fold_in(key, 11)
    keys = jax.random.split(inner_key, 7)
    rate = jnp.exp(jax.random.uniform(keys[0], (HEADS,), jnp.float32, math.log(0.5), math.log(2.0)))
    slow = jax.random.uniform(keys[1], (HEADS,), jnp.float32) < 0.5
    fast_target = jnp.exp(jax.random.uniform(keys[2], (HEADS,), jnp.float32, math.log(0.003), math.log(0.04)))
    slow_target = jnp.exp(jax.random.uniform(keys[3], (HEADS,), jnp.float32, math.log(0.0002), math.log(0.0009)))
    desired_quantity = jnp.where(slow, slow_target, fast_target)
    rough_guess = jnp.exp(jax.random.uniform(keys[4], (SAMPLES_OVERALL, HEADS), jnp.float32, math.log(0.5), math.log(2.0)))
    location_sequence = jax.random.randint(keys[5], (3,), 0, SAMPLES_OVERALL)
    amplitude_measure = jnp.exp(jax.random.uniform(keys[6], (3,), jnp.float32, math.log(0.22), math.log(0.7)))
    spike_duration = jnp.zeros((SAMPLES_OVERALL,), jnp.float32).at[location_sequence].set(amplitude_measure)
    logarithmic_increment = desired_quantity[None, :] * rough_guess + spike_duration[:, None]
    return (rate, logarithmic_increment / rate[None, :])


def draw_decay_rate(key, part):
    return rates_and_steps(key)[0]


def draw_step_size(key, part):
    return rates_and_steps(key)[1]


def draw_code_index(key, part):
    inner_key = jax.random.fold_in(key, 23)
    keys = jax.random.split(inner_key, 3)
    per_device = FRAMES_DEV // N_CHAN * GROUPS
    shard_size = CODES // N_CHAN
    shifts = jax.random.randint(keys[0], (N_SEQ, 1, 1), 0, N_CHAN)
    base = (jnp.arange(per_device, dtype=jnp.int32)[None, None, :] + shifts) % N_CHAN
    base = jnp.broadcast_to(base, (N_SEQ, N_CHAN, per_device))
    perm_keys = jax.random.split(keys[1], N_SEQ * N_CHAN)
    orders = jax.vmap(lambda one_key: jax.random.permutation(one_key, per_device))(perm_keys)
    orders = orders.reshape(N_SEQ, N_CHAN, per_device).astype(jnp.int32)
    owners = jnp.take_along_axis(base, orders, axis=2)
    within = jax.random.randint(keys[2], owners.shape, 0, shard_size)
    return (owners * shard_size + within).reshape(SAMPLES_OVERALL, GROUPS).astype(jnp.int32)


def block_scale(own_key, dims, pieces, low, high):
    loudness = 1.0
    for axis_at, parts in pieces:
        draws = jax.random.uniform(jax.random.fold_in(jax.random.fold_in(own_key, 6), axis_at), (parts,), jnp.float32, low / len(pieces), high / len(pieces))
        loudness = loudness * jnp.repeat(jnp.exp(draws), dims[axis_at] // parts).reshape((-1,) + (1,) * (len(dims) - 1 - axis_at))
    return loudness


def bell_draw(rng, shape, scale, most, pieces=(), held_as=jnp.bfloat16):
    factor_of = block_scale(rng, shape, pieces, -0.22, 0.18) if pieces else 1.0
    drawn = jax.random.normal(rng, shape, jnp.float32) * scale * factor_of
    return jnp.minimum(jnp.maximum(drawn, -most), most).astype(held_as)


def setup_inputs(seed: int = 0) -> dict:
    key_of = jax.random.split(jax.random.key(seed), 12)
    frames_in = bell_draw(key_of[0], (SAMPLES_OVERALL, INNER), 1.0, 6.0, ((0, 4), (1, 8)))
    gate_in = bell_draw(key_of[1], (SAMPLES_OVERALL, INNER), 1.0, 6.0, ((0, 4), (1, 8)))
    in_keys = bell_draw(key_of[2], (SAMPLES_OVERALL, STATE), 1.0, 6.0, ((0, 4),))
    out_keys = bell_draw(key_of[3], (SAMPLES_OVERALL, STATE), 1.0, 6.0, ((0, 4),))
    step_size = draw_step_size(jax.random.fold_in(key_of[11], 71), 0)
    decay_rate = draw_decay_rate(jax.random.fold_in(key_of[11], 71), 0)
    skip_gain = jnp.clip(jnp.exp(math.log(2.0) - 1.3862944 * jax.random.uniform(key_of[6], (HEADS,), jnp.float32) ** block_scale(key_of[6], (HEADS,), ((0, 8),), -0.2, 0.2)), 0.5, 2.0)
    out_weight = bell_draw(key_of[7], (INNER, D), INNER ** -0.5, 0.09375, ((0, 8),))
    codebook = bell_draw(key_of[8], (CODES, CODE_DIM), 1.0, 6.0, ((0, 8),))
    code_index = draw_code_index(jax.random.fold_in(key_of[11], 71), 0)
    upstream = bell_draw(key_of[10], (SAMPLES_OVERALL, D), 1.0, 6.0, ((0, 32),))
    return dict(frames_in=frames_in, gate_in=gate_in, in_keys=in_keys, out_keys=out_keys, step_size=step_size, decay_rate=decay_rate, skip_gain=skip_gain, out_weight=out_weight, codebook=codebook, code_index=code_index, upstream=upstream)


commit_weight = 0.25

def group_norm(v):
    return jnp.sqrt(lax.optimization_barrier(jnp.sum(v * v, axis=-1, keepdims=True)) + 1e-06)

def rotate_back(e, q, g):
    ne = group_norm(e)
    nq = group_norm(q)
    eh = e / ne
    qh = q / nq
    summed = eh + qh
    unit = summed / group_norm(summed)
    scale = nq / ne
    along = lax.optimization_barrier(jnp.sum(unit * g, axis=-1, keepdims=True))
    toward = lax.optimization_barrier(jnp.sum(qh * g, axis=-1, keepdims=True))
    return scale * (g - 2.0 * unit * along + 2.0 * eh * toward) + 2.0 * commit_weight * (e - q)

def reference(frames_in, gate_in, in_keys, out_keys, step_size, decay_rate, skip_gain, out_weight, codebook, code_index, upstream):
    highest = lax.Precision.HIGHEST
    blocks = SAMPLES_OVERALL // BLOCK
    xs = frames_in.astype(jnp.float32).reshape(blocks, BLOCK, HEADS, HEAD_DIM)
    dts = step_size.reshape(blocks, BLOCK, HEADS)
    bks = in_keys.astype(jnp.float32).reshape(blocks, BLOCK, STATE)
    cks = out_keys.astype(jnp.float32).reshape(blocks, BLOCK, STATE)
    lower = jnp.arange(BLOCK)[:, None] >= jnp.arange(BLOCK)[None, :]

    def block_step(state, inputs):
        xb, dtb, bb, cb = inputs
        cums = jnp.cumsum(-dtb * decay_rate[None, :], axis=0)
        trans = cums.T
        spread = jnp.where(lower[None], trans[:, :, None] - trans[:, None, :], 0.0)
        masks = jnp.where(lower[None], jnp.exp(spread), 0.0)
        gram = jnp.dot(cb, bb.T, precision=highest)
        inputs_scaled = dtb[:, :, None] * xb
        intra = jnp.einsum('hij,jhp->ihp', masks * gram[None], inputs_scaled, precision=highest)
        inter = jnp.exp(cums)[:, :, None] * jnp.einsum('in,hpn->ihp', cb, state, precision=highest)
        weight = jnp.exp(cums[-1][None, :] - cums)
        fresh = jnp.einsum('jh,jhp,jn->hpn', weight, inputs_scaled, bb, precision=highest)
        updated = jnp.exp(cums[-1])[:, None, None] * state + fresh
        return (updated, intra + inter + skip_gain[None, :, None] * xb)
    start = jnp.zeros((HEADS, HEAD_DIM, STATE), jnp.float32)
    _, mixed = lax.scan(block_step, start, (xs, dts, bks, cks))
    mixed = mixed.reshape(SAMPLES_OVERALL, INNER)
    gated = (mixed * jax.nn.silu(gate_in.astype(jnp.float32))).astype(jnp.bfloat16)
    latent = jnp.dot(gated, out_weight, preferred_element_type=jnp.float32).astype(jnp.bfloat16)
    e = latent.astype(jnp.float32).reshape(SAMPLES_OVERALL, GROUPS, CODE_DIM)
    q = jnp.take(codebook, code_index, axis=0).astype(jnp.float32)
    g = upstream.astype(jnp.float32).reshape(SAMPLES_OVERALL, GROUPS, CODE_DIM)
    latent_grad = rotate_back(e, q, g).reshape(SAMPLES_OVERALL, D)
    diff = (q - e).astype(jnp.bfloat16)
    table = jnp.zeros((CODES, CODE_DIM), jnp.float32).at[code_index.reshape(-1)].add(diff.reshape(-1, CODE_DIM).astype(jnp.float32))
    return (latent, latent_grad, 2.0 * table)
```

```python
import functools

import jax
import jax.numpy as jnp
from jax import lax
from jax.experimental import pallas as pl
from jax.experimental.pallas import tpu as pltpu
from jax.sharding import PartitionSpec as P

COMMIT = 0.25
CODE_BLOCK = 256
F32 = jnp.float32
BF16 = jnp.bfloat16
HIGHEST = lax.Precision.HIGHEST


def flip(x, axis, bit):
    n = lax.axis_size(axis)
    return lax.ppermute(x, axis, [(i, i ^ bit) for i in range(n)])


def dot_nt(a, b):
    return lax.dot_general(a, b, (((1,), (1,)), ((), ())), preferred_element_type=F32)


def dot_tn(a, b):
    return lax.dot_general(a, b, (((0,), (0,)), ((), ())), preferred_element_type=F32)


def per_head(values, heads, width):
    rows = values.shape[0]
    return jnp.concatenate(
        [jnp.broadcast_to(values[:, h : h + 1], (rows, width)) for h in range(heads)], axis=1
    )


def states_kernel(
    x_ref, b_ref, dt_ref, rate_ref,
    starts_ref, cums_ref, cums_t_ref, before_ref, final_ref, total_ref,
    state, seen,
):
    step = pl.program_id(0)
    rows, width = x_ref.shape
    heads = dt_ref.shape[1]
    head_dim = width // heads

    @pl.when(step == 0)
    def _():
        state[...] = jnp.zeros_like(state)
        seen[...] = jnp.zeros_like(seen)

    dt = dt_ref[...]
    logs = -dt * rate_ref[...]
    lower = (
        lax.broadcasted_iota(jnp.int32, (rows, rows), 0)
        >= lax.broadcasted_iota(jnp.int32, (rows, rows), 1)
    ).astype(F32)
    cums = jnp.dot(lower, logs, precision=HIGHEST, preferred_element_type=F32)
    cums_ref[...] = cums
    cums_t_ref[0] = cums.T
    before_ref[0] = seen[...]
    total = cums[rows - 1 : rows, :]
    weight = dt * jnp.exp(total - cums)
    xw = (x_ref[...].astype(F32) * per_head(weight, heads, head_dim)).astype(BF16)
    fresh = dot_tn(xw, b_ref[...])
    starts_ref[0] = state[...]
    keep = jnp.exp(total)
    for h in range(heads):
        rs = slice(h * head_dim, (h + 1) * head_dim)
        state[rs, :] = state[rs, :] * keep[:, h : h + 1] + fresh[rs, :]
    seen[...] = seen[...] + total

    @pl.when(step == pl.num_programs(0) - 1)
    def _():
        final_ref[...] = state[...]
        total_ref[...] = seen[...]


def block_states(frames_in, in_keys, step_size, rate, rows):
    frames, width = frames_in.shape
    nstate = in_keys.shape[1]
    heads = step_size.shape[1]
    nb = frames // rows
    return pl.pallas_call(
        states_kernel,
        grid=(nb,),
        in_specs=[
            pl.BlockSpec((rows, width), lambda i: (i, 0)),
            pl.BlockSpec((rows, nstate), lambda i: (i, 0)),
            pl.BlockSpec((rows, heads), lambda i: (i, 0)),
            pl.BlockSpec((1, heads), lambda i: (0, 0)),
        ],
        out_specs=[
            pl.BlockSpec((1, width, nstate), lambda i: (i, 0, 0)),
            pl.BlockSpec((rows, heads), lambda i: (i, 0)),
            pl.BlockSpec((1, heads, rows), lambda i: (i, 0, 0)),
            pl.BlockSpec((1, 1, heads), lambda i: (i, 0, 0)),
            pl.BlockSpec((width, nstate), lambda i: (0, 0)),
            pl.BlockSpec((1, heads), lambda i: (0, 0)),
        ],
        out_shape=[
            jax.ShapeDtypeStruct((nb, width, nstate), F32),
            jax.ShapeDtypeStruct((frames, heads), F32),
            jax.ShapeDtypeStruct((nb, heads, rows), F32),
            jax.ShapeDtypeStruct((nb, 1, heads), F32),
            jax.ShapeDtypeStruct((width, nstate), F32),
            jax.ShapeDtypeStruct((1, heads), F32),
        ],
        scratch_shapes=[pltpu.VMEM((width, nstate), F32), pltpu.VMEM((1, heads), F32)],
        name="block_states",
    )(frames_in, in_keys, step_size, rate)


def intra_kernel(x_ref, b_ref, c_ref, dt_ref, cums_ref, cums_t_ref, skip_ref, out_ref):
    rows, width = x_ref.shape
    heads = dt_ref.shape[1]
    head_dim = width // heads
    tile = min(rows, 128)
    cums = cums_ref[...]
    cums_t = cums_t_ref[0]
    x = x_ref[...].astype(F32)
    xdt = (x * per_head(dt_ref[...], heads, head_dim)).astype(BF16)
    skipped = x * per_head(skip_ref[...], heads, head_dim)
    for t in range(rows // tile):
        rs = slice(t * tile, (t + 1) * tile)
        n = (t + 1) * tile
        gram = dot_nt(c_ref[rs, :], b_ref[0:n, :])
        allowed = (
            lax.broadcasted_iota(jnp.int32, (tile, n), 0) + t * tile
            >= lax.broadcasted_iota(jnp.int32, (tile, n), 1)
        )
        parts = []
        for h in range(heads):
            spread = cums[rs, h : h + 1] - cums_t[h : h + 1, 0:n]
            mask = jnp.exp(jnp.where(allowed, spread, -1e30))
            parts.append(
                jnp.dot(
                    (mask * gram).astype(BF16),
                    xdt[0:n, h * head_dim : (h + 1) * head_dim],
                    preferred_element_type=F32,
                )
            )
        out_ref[rs, :] = jnp.concatenate(parts, axis=1) + skipped[rs, :]


def intra_block(frames_in, in_keys, out_keys, step_size, cums, cums_t, skip, rows):
    frames, width = frames_in.shape
    nstate = in_keys.shape[1]
    heads = step_size.shape[1]
    return pl.pallas_call(
        intra_kernel,
        grid=(frames // rows,),
        in_specs=[
            pl.BlockSpec((rows, width), lambda i: (i, 0)),
            pl.BlockSpec((rows, nstate), lambda i: (i, 0)),
            pl.BlockSpec((rows, nstate), lambda i: (i, 0)),
            pl.BlockSpec((rows, heads), lambda i: (i, 0)),
            pl.BlockSpec((rows, heads), lambda i: (i, 0)),
            pl.BlockSpec((1, heads, rows), lambda i: (i, 0, 0)),
            pl.BlockSpec((1, heads), lambda i: (0, 0)),
        ],
        out_specs=pl.BlockSpec((rows, width), lambda i: (i, 0)),
        out_shape=jax.ShapeDtypeStruct((frames, width), F32),
        name="intra_block",
    )(frames_in, in_keys, out_keys, step_size, cums, cums_t, skip)


def gate_kernel(
    order_ref, mixed_ref, gate_ref, c_ref, cums_ref, starts_ref, before_ref, incoming_ref, out_ref
):
    rows, width = mixed_ref.shape
    heads = cums_ref.shape[1]
    head_dim = width // heads
    carry = jnp.exp(before_ref[0])
    parts = []
    for h in range(heads):
        rs = slice(h * head_dim, (h + 1) * head_dim)
        parts.append(starts_ref[0, rs, :] + incoming_ref[rs, :] * carry[:, h : h + 1])
    start = jnp.concatenate(parts, axis=0).astype(BF16)
    inter = dot_nt(c_ref[...], start)
    mixed = mixed_ref[...] + inter * per_head(jnp.exp(cums_ref[...]), heads, head_dim)
    gate = gate_ref[...].astype(F32)
    gated = (mixed * (gate / (1.0 + jnp.exp(-gate)))).astype(BF16)
    second = order_ref[order_ref.shape[0] - 1] == 1
    half = width // 2
    lo = gated[:, :half]
    hi = gated[:, half:]
    out_ref[0, :, :half] = jnp.where(second, hi, lo)
    out_ref[0, :, half:] = jnp.where(second, lo, hi)


def gated_blocks(order, count, mixed, gate_in, out_keys, cums, starts, before, incoming, rows):
    width = mixed.shape[1]
    nstate = out_keys.shape[1]
    heads = cums.shape[1]
    return pl.pallas_call(
        gate_kernel,
        grid_spec=pltpu.PrefetchScalarGridSpec(
            num_scalar_prefetch=1,
            grid=(count,),
            in_specs=[
                pl.BlockSpec((rows, width), lambda i, o: (o[i], 0)),
                pl.BlockSpec((rows, width), lambda i, o: (o[i], 0)),
                pl.BlockSpec((rows, nstate), lambda i, o: (o[i], 0)),
                pl.BlockSpec((rows, heads), lambda i, o: (o[i], 0)),
                pl.BlockSpec((1, width, nstate), lambda i, o: (o[i], 0, 0)),
                pl.BlockSpec((1, 1, heads), lambda i, o: (o[i], 0, 0)),
                pl.BlockSpec((width, nstate), lambda i, o: (0, 0)),
            ],
            out_specs=pl.BlockSpec((1, rows, width), lambda i, o: (i, 0, 0)),
        ),
        out_shape=jax.ShapeDtypeStruct((count, rows, width), BF16),
        name="gated_blocks",
    )(order, mixed, gate_in, out_keys, cums, starts, before, incoming)


def project_kernel(*refs, count, added):
    gs = refs[:count]
    firsts = refs[count : 2 * count]
    seconds = refs[2 * count : 3 * count]
    out_ref = refs[-1]
    half = firsts[0].shape[0]
    acc = None
    for g, a, b in zip(gs, firsts, seconds):
        part = jnp.dot(g[:, :half], a[...], preferred_element_type=F32)
        part = part + jnp.dot(g[:, half:], b[...], preferred_element_type=F32)
        acc = part if acc is None else acc + part
    if added:
        acc = acc + refs[3 * count][...].astype(F32)
    out_ref[...] = acc.astype(BF16)


def project(gs, firsts, seconds, add=None):
    count = len(gs)
    rows, width = gs[0].shape
    half, cols = firsts[0].shape
    tile = min(cols, 512)
    in_specs = [pl.BlockSpec((rows, width), lambda j: (0, 0))] * count
    in_specs += [pl.BlockSpec((half, tile), lambda j: (0, j))] * (2 * count)
    args = list(gs) + list(firsts) + list(seconds)
    if add is not None:
        in_specs.append(pl.BlockSpec((rows, tile), lambda j: (0, j)))
        args.append(add)
    return pl.pallas_call(
        functools.partial(project_kernel, count=count, added=add is not None),
        grid=(cols // tile,),
        in_specs=in_specs,
        out_specs=pl.BlockSpec((rows, tile), lambda j: (0, j)),
        out_shape=jax.ShapeDtypeStruct((rows, cols), BF16),
        name="project",
    )(*args)


def diff_kernel(pos_ref, latent_ref, q_ref, out_ref):
    _, slots, dim = out_ref.shape
    groups, rows = pos_ref.shape
    base = pl.program_id(0) * slots
    slot = lax.broadcasted_iota(jnp.int32, (slots, rows), 0) + base
    acc = None
    for g in range(groups):
        pick = jnp.where(slot == pos_ref[g : g + 1, :], 1.0, 0.0).astype(BF16)
        part = jnp.dot(
            pick, latent_ref[:, g * dim : (g + 1) * dim], preferred_element_type=F32
        )
        acc = part if acc is None else acc + part
    out_ref[0] = (q_ref[0].astype(F32) - acc).astype(BF16)


def diffs(pos, latent, q):
    count, slots, dim = q.shape
    return pl.pallas_call(
        diff_kernel,
        grid=(count,),
        in_specs=[
            pl.BlockSpec(pos.shape, lambda i: (0, 0)),
            pl.BlockSpec(latent.shape, lambda i: (0, 0)),
            pl.BlockSpec((1, slots, dim), lambda i: (i, 0, 0)),
        ],
        out_specs=pl.BlockSpec((1, slots, dim), lambda i: (i, 0, 0)),
        out_shape=jax.ShapeDtypeStruct(q.shape, BF16),
        name="diffs",
    )(pos, latent, q)


def norm_of(v):
    return jnp.sqrt(jnp.sum(v * v, axis=-1, keepdims=True) + 1e-06)


def grad_kernel(pos_ref, latent_ref, up_ref, q_ref, out_ref):
    entries, dim = q_ref.shape
    rows = latent_ref.shape[0]
    groups = latent_ref.shape[1] // dim
    slot = lax.broadcasted_iota(jnp.int32, (rows, entries), 1)
    for n in range(groups):
        cols = slice(n * dim, (n + 1) * dim)
        pick = jnp.where(slot == pos_ref[:, n : n + 1], 1.0, 0.0).astype(BF16)
        q = jnp.dot(pick, q_ref[...], preferred_element_type=F32)
        e = latent_ref[:, cols].astype(F32)
        g = up_ref[:, cols].astype(F32)
        ne = norm_of(e)
        nq = norm_of(q)
        eh = e / ne
        qh = q / nq
        summed = eh + qh
        unit = summed / norm_of(summed)
        along = jnp.sum(unit * g, axis=-1, keepdims=True)
        toward = jnp.sum(qh * g, axis=-1, keepdims=True)
        out_ref[:, cols] = (nq / ne) * (g - 2.0 * unit * along + 2.0 * eh * toward) + (
            2.0 * COMMIT
        ) * (e - q)


def latent_grads(pos_cols, latent, upstream, q):
    rows, width = latent.shape
    groups = pos_cols.shape[1]
    tile = min(rows, 64)
    return pl.pallas_call(
        grad_kernel,
        grid=(rows // tile,),
        in_specs=[
            pl.BlockSpec((tile, groups), lambda i: (i, 0)),
            pl.BlockSpec((tile, width), lambda i: (i, 0)),
            pl.BlockSpec((tile, width), lambda i: (i, 0)),
            pl.BlockSpec(q.shape, lambda i: (0, 0)),
        ],
        out_specs=pl.BlockSpec((tile, width), lambda i: (i, 0)),
        out_shape=jax.ShapeDtypeStruct((rows, width), F32),
        name="latent_grads",
    )(pos_cols, latent, upstream, q)


def order_kernel(*refs):
    place_ref = refs[0]
    chunks = refs[1:-1]
    out_ref = refs[-1]
    tile = out_ref.shape[0]
    slots = chunks[0].shape[0]
    slot = lax.broadcasted_iota(jnp.int32, (tile, slots), 0) + pl.program_id(0) * tile
    acc = None
    for n, chunk in enumerate(chunks):
        pick = jnp.where(slot == place_ref[:, n * slots : (n + 1) * slots], 1.0, 0.0).astype(BF16)
        part = jnp.dot(pick, chunk[...], preferred_element_type=F32)
        acc = part if acc is None else acc + part
    out_ref[...] = acc.astype(BF16)


def ordered(place, chunks):
    slots, dim = chunks[0].shape
    total = slots * len(chunks)
    tile = min(total, 256)
    return pl.pallas_call(
        order_kernel,
        grid=(total // tile,),
        in_specs=[pl.BlockSpec((1, total), lambda i: (0, 0))]
        + [pl.BlockSpec((slots, dim), lambda i: (0, 0))] * len(chunks),
        out_specs=pl.BlockSpec((tile, dim), lambda i: (i, 0)),
        out_shape=jax.ShapeDtypeStruct((total, dim), BF16),
        name="ordered",
    )(place, *chunks)


def table_kernel(bounds_ref, codes_ref, *refs, window):
    runs = refs[:-1]
    out_ref = refs[-1]
    codes, dim = out_ref.shape
    length = runs[0].shape[0]
    block = pl.program_id(0)
    base = block * codes
    lane = lax.broadcasted_iota(jnp.int32, (window, 128), 1) + base
    row = lax.broadcasted_iota(jnp.int32, (window, 128), 0)

    def gathered(turn):
        picks = []
        rows = []
        for r, run in enumerate(runs):
            first = (bounds_ref[r, block] // 16) * 16 + turn * window
            at = pl.multiple_of(jnp.minimum(first, length - window), 16)
            mine = codes_ref[r, pl.ds(at, window), :]
            mine = jnp.where(row + at >= first, mine, -1)
            picks.append(
                jnp.concatenate(
                    [
                        jnp.where(mine == lane + n * 128, 1.0, 0.0).astype(BF16)
                        for n in range(codes // 128)
                    ],
                    axis=1,
                )
            )
            rows.append(run[pl.ds(at, window), :])
        pick = jnp.concatenate(picks, axis=0)
        values = jnp.concatenate(rows, axis=0)
        return 2.0 * dot_tn(pick, values)

    out_ref[...] = gathered(0)
    turns = 0
    for r in range(len(runs)):
        lo = (bounds_ref[r, block] // 16) * 16
        hi = bounds_ref[r, block + 1]
        turns = jnp.maximum(turns, (hi - lo + window - 1) // window)

    def more(turn, carry):
        out_ref[...] += gathered(turn)
        return carry

    lax.fori_loop(1, turns, more, 0)


def table(bounds, codes, runs, codes_dev):
    length, dim = runs[0].shape
    block = min(CODE_BLOCK, codes_dev)
    blocks = codes_dev // block
    window = 16
    while window < length and window < 2 * length // blocks:
        window *= 2
    return pl.pallas_call(
        functools.partial(table_kernel, window=window),
        grid_spec=pltpu.PrefetchScalarGridSpec(
            num_scalar_prefetch=1,
            grid=(blocks,),
            in_specs=[pl.BlockSpec(codes.shape, lambda i, b: (0, 0, 0))]
            + [pl.BlockSpec((length, dim), lambda i, b: (0, 0))] * len(runs),
            out_specs=pl.BlockSpec((block, dim), lambda i, b: (i, 0)),
        ),
        out_shape=jax.ShapeDtypeStruct((codes_dev, dim), F32),
        name="table",
    )(bounds, codes, *runs)


def body(
    frames_in,
    gate_in,
    in_keys,
    out_keys,
    step_size,
    decay_rate,
    skip_gain,
    out_weight,
    codebook,
    code_index,
    upstream,
):
    chans = lax.axis_size("chan")
    seqs = lax.axis_size("seq")
    chan = lax.axis_index("chan")
    seq = lax.axis_index("seq")
    half = chans // 2
    core = seq % 2
    frames, width = frames_in.shape
    rows = frames // chans
    codes_dev, dim = codebook.shape
    groups = code_index.shape[1]
    heads = decay_rate.shape[0]
    nstate = in_keys.shape[1]

    wrows = out_weight.shape[0] // 2
    mine = lax.dynamic_slice_in_dim(out_weight, core * wrows, wrows, 0)
    other = lax.dynamic_slice_in_dim(out_weight, (1 - core) * wrows, wrows, 0)
    firsts = [mine] + [flip(mine, "chan", k) for k in range(1, half)]
    seconds = [other] + [flip(firsts[k], "seq", 1) for k in range(1, half)]

    rate = decay_rate.reshape(1, heads)
    starts, cums, cums_t, before, final, total = block_states(
        frames_in, in_keys, step_size, rate, rows
    )
    mixed = intra_block(
        frames_in, in_keys, out_keys, step_size, cums, cums_t, skip_gain.reshape(1, heads), rows
    )
    head_dim = width // heads
    held = final
    held_log = total
    incoming = jnp.zeros_like(final)
    lower_log = jnp.zeros_like(total)

    def rows_of(logs):
        return jnp.broadcast_to(
            jnp.exp(logs).reshape(heads, 1, 1), (heads, head_dim, 1)
        ).reshape(width, 1)

    bit = 1
    while bit < seqs:
        got = flip(held.astype(BF16), "seq", bit).astype(F32)
        got_log = flip(held_log, "seq", bit)
        after = (seq & bit) != 0
        incoming = jnp.where(after, incoming + rows_of(lower_log) * got, incoming)
        lower_log = jnp.where(after, lower_log + got_log, lower_log)
        held = jnp.where(
            after, rows_of(held_log) * got + held, rows_of(got_log) * held + got
        )
        held_log = held_log + got_log
        bit *= 2

    top = chan // half
    low = chan % half
    turn = jnp.arange(half, dtype=jnp.int32)
    near = top * half + (low ^ turn)
    far = (1 - top) * half + (low ^ turn)
    tail = core.astype(jnp.int32)[None]

    def gated_for(which):
        out = gated_blocks(
            jnp.concatenate([which.astype(jnp.int32), tail]),
            half, mixed, gate_in, out_keys, cums, starts, before, incoming, rows,
        )
        return [out[0]] + [flip(out[k], "chan", k) for k in range(1, half)]

    across = flip(project(gated_for(far), firsts, seconds), "chan", half)
    near_blocks = gated_for(near)

    entries = rows * groups
    slots = max(1, (entries + chans - 1) // chans)
    index_t = code_index.T
    flat = index_t.reshape(entries)
    owner = flat // codes_dev
    within = flat - owner * codes_dev
    hot = (owner[:, None] == jnp.arange(chans, dtype=jnp.int32)[None, :]).astype(BF16)
    entry = jnp.arange(entries, dtype=jnp.int32)
    earlier = (entry[:, None] > entry[None, :]).astype(BF16)
    counts = jnp.dot(earlier, hot, preferred_element_type=F32)
    rank = jnp.sum(counts * hot.astype(F32), axis=1).astype(jnp.int32)
    slot_of = owner * slots + rank
    place = (owner ^ chan) * slots + rank
    pos = place.reshape(groups, rows)
    wanted = jnp.sum(
        jnp.where(slot_of[None, :] == entry[:, None], within[None, :] + 1, 0), axis=1
    )
    wanted = jnp.where(wanted == 0, codes_dev, wanted - 1).reshape(chans, slots)
    received = lax.all_to_all(wanted, "chan", split_axis=0, concat_axis=0, tiled=True)
    lane = jnp.arange(chans, dtype=jnp.int32)
    turned = (lane[:, None] ^ chan) == lane[None, :]
    asked = jnp.sum(jnp.where(turned[:, :, None], received[None], 0), axis=1)
    picked = jnp.take(codebook, jnp.minimum(asked, codes_dev - 1), axis=0)
    q = jnp.stack([picked[0]] + [flip(picked[k], "chan", k) for k in range(1, chans)])

    asked_runs = asked.reshape(1, entries)
    bit = seqs // 2
    while bit > 1:
        asked_runs = jnp.concatenate([asked_runs, flip(asked_runs, "seq", bit)])
        bit //= 2
    keys = asked_runs * entries + entry[None, :]
    ranks = jnp.sum((keys[:, None, :] < keys[:, :, None]).astype(jnp.int32), axis=2)
    run_codes = jnp.sum(
        jnp.where(ranks[:, None, :] == entry[None, :, None], asked_runs[:, None, :], 0), axis=2
    )
    if seqs > 1:
        run_codes = jnp.concatenate([run_codes, flip(run_codes, "seq", 1)])
    block = min(CODE_BLOCK, codes_dev)
    edges = jnp.arange(codes_dev // block + 1, dtype=jnp.int32) * block
    bounds = jnp.sum((run_codes[:, None, :] < edges[None, :, None]).astype(jnp.int32), axis=2)
    codes_wide = jnp.broadcast_to(run_codes[:, :, None], run_codes.shape + (128,))

    latent = project(near_blocks, firsts, seconds, across)

    diff = diffs(pos, latent, q)
    chunks = []
    for k in range(chans):
        got = [diff[k] if k == 0 else flip(diff[k], "chan", k)]
        bit = seqs // 2
        while bit > 1:
            got = got + [flip(a, "seq", bit) for a in got]
            bit //= 2
        chunks.append(got)
    latent_grad = latent_grads(pos.T, latent, upstream, q.reshape(entries, dim))
    runs = [
        ordered(ranks[r : r + 1], [chunks[k][r] for k in range(chans)])
        for r in range(max(1, seqs // 2))
    ]
    if seqs > 1:
        runs = runs + [flip(a, "seq", 1) for a in runs]
    codebook_grad = table(bounds, codes_wide, runs, codes_dev)
    return (latent, latent_grad, codebook_grad)


def solution(mesh):
    placed = (
        P("seq", "chan"),
        P("seq", "chan"),
        P("seq", None),
        P("seq", None),
        P("seq", "chan"),
        P("chan"),
        P("chan"),
        P("chan", None),
        P("chan", None),
        P(("seq", "chan"), None),
        P(("seq", "chan"), None),
    )
    return jax.shard_map(
        body,
        mesh=mesh,
        in_specs=placed,
        out_specs=(P(("seq", "chan"), None), P(("seq", "chan"), None), P("chan", None)),
        check_vma=False,
    )
```

```python
import functools

import jax
import jax.numpy as jnp
from jax import lax
from jax.experimental import pallas as pl
from jax.experimental.pallas import tpu as pltpu
from jax.sharding import PartitionSpec as P


COMMIT = 0.25
CODE_BLOCK = 256
F32 = jnp.float32
BF16 = jnp.bfloat16


def flip(x, axis, bit):
    n = lax.axis_size(axis)
    return lax.ppermute(x, axis, [(i, i ^ bit) for i in range(n)])


def dot_nt(a, b):
    return lax.dot_general(a, b, (((1,), (1,)), ((), ())), preferred_element_type=F32)


def per_head(values, heads, width):
    rows = values.shape[0]
    return jnp.concatenate(
        [jnp.broadcast_to(values[:, h : h + 1], (rows, width)) for h in range(heads)], axis=1
    )


def states_kernel(
    x_ref, b_ref, dt_ref, rate_ref, starts_ref, cums_ref, before_ref, final_ref, sent_ref,
    state, seen, upper,
):
    step = pl.program_id(0)
    rows, width = x_ref.shape
    heads = dt_ref.shape[0]
    head_dim = width // heads

    @pl.when(step == 0)
    def _():
        state[...] = jnp.zeros_like(state)
        seen[...] = jnp.zeros_like(seen)
        upper[...] = jnp.where(
            lax.broadcasted_iota(jnp.int32, (rows, rows), 0)
            <= lax.broadcasted_iota(jnp.int32, (rows, rows), 1),
            1.0,
            0.0,
        ).astype(BF16)

    dt = dt_ref[...]
    logs = -dt * rate_ref[...]
    one = logs.astype(BF16).astype(F32)
    two = (logs - one).astype(BF16).astype(F32)
    three = logs - one - two
    terms = jnp.concatenate([one, two, three, jnp.zeros_like(one)], axis=0).astype(BF16)
    sums = jnp.dot(terms, upper[...], preferred_element_type=F32)
    cums = sums[:heads] + sums[heads : 2 * heads] + sums[2 * heads : 3 * heads]
    cums_ref[...] = cums
    before_ref[0] = seen[...]
    total = cums[:, rows - 1 : rows]
    weight = dt * jnp.exp(total - cums)
    x_t = x_ref[...].T
    scaled = jnp.concatenate(
        [
            (x_t[h * head_dim : (h + 1) * head_dim, :].astype(F32) * weight[h : h + 1, :]).astype(
                BF16
            )
            for h in range(heads)
        ],
        axis=0,
    )
    fresh = jnp.dot(scaled, b_ref[...], preferred_element_type=F32)
    starts_ref[0] = state[...].astype(BF16)
    keep = jnp.exp(jnp.broadcast_to(total, seen.shape))
    for h in range(heads):
        rs = slice(h * head_dim, (h + 1) * head_dim)
        state[rs, :] = state[rs, :] * keep[h : h + 1, :] + fresh[rs, :]
    seen[...] = seen[...] + total

    @pl.when(step == pl.num_programs(0) - 1)
    def _():
        final_ref[...] = state[...]
        sent_ref[...] = state[...].astype(BF16)


def block_states(frames_in, in_keys, step_t, rate, rows):
    frames, width = frames_in.shape
    nstate = in_keys.shape[1]
    heads = step_t.shape[0]
    nb = frames // rows
    return pl.pallas_call(
        states_kernel,
        grid=(nb,),
        in_specs=[
            pl.BlockSpec((rows, width), lambda i: (i, 0)),
            pl.BlockSpec((rows, nstate), lambda i: (i, 0)),
            pl.BlockSpec((heads, rows), lambda i: (0, i)),
            pl.BlockSpec((heads, 1), lambda i: (0, 0)),
        ],
        out_specs=[
            pl.BlockSpec((1, width, nstate), lambda i: (i, 0, 0)),
            pl.BlockSpec((heads, rows), lambda i: (0, i)),
            pl.BlockSpec((1, heads, nstate), lambda i: (i, 0, 0)),
            pl.BlockSpec((width, nstate), lambda i: (0, 0)),
            pl.BlockSpec((width, nstate), lambda i: (0, 0)),
        ],
        out_shape=[
            jax.ShapeDtypeStruct((nb, width, nstate), BF16),
            jax.ShapeDtypeStruct((heads, frames), F32),
            jax.ShapeDtypeStruct((nb, heads, nstate), F32),
            jax.ShapeDtypeStruct((width, nstate), F32),
            jax.ShapeDtypeStruct((width, nstate), BF16),
        ],
        scratch_shapes=[
            pltpu.VMEM((width, nstate), F32),
            pltpu.VMEM((heads, nstate), F32),
            pltpu.VMEM((rows, rows), BF16),
        ],
        name="block_states",
    )(frames_in, in_keys, step_t, rate)


def intra_kernel(
    order_ref, x_ref, gate_ref, b_ref, c_ref, dt_ref, cums_ref, skip_ref, base_ref, slope_ref
):
    rows, width = x_ref.shape
    heads = dt_ref.shape[0]
    head_dim = width // heads
    tile = min(rows, 128)
    cums_t = cums_ref[...]
    cums = cums_t.T
    dt = dt_ref[...]
    for t in range(rows // tile):
        rs = slice(t * tile, (t + 1) * tile)
        n = (t + 1) * tile
        gram = dot_nt(c_ref[rs, :], b_ref[0:n, :])
        allowed = (
            lax.broadcasted_iota(jnp.int32, (tile, n), 0) + t * tile
            >= lax.broadcasted_iota(jnp.int32, (tile, n), 1)
        )
        parts = []
        for h in range(heads):
            spread = cums[rs, h : h + 1] - cums_t[h : h + 1, 0:n]
            mask = jnp.exp(jnp.where(allowed, spread, -1e30)) * dt[h : h + 1, 0:n]
            parts.append(
                jnp.dot(
                    (mask * gram).astype(BF16),
                    x_ref[0:n, h * head_dim : (h + 1) * head_dim],
                    preferred_element_type=F32,
                )
            )
        gate = gate_ref[rs, :].astype(F32)
        gate = gate / (1.0 + jnp.exp(-gate))
        mixed = jnp.concatenate(parts, axis=1) + x_ref[rs, :].astype(F32) * skip_ref[...]
        base_ref[0, rs, :] = mixed * gate
        slope_ref[0, rs, :] = (gate * per_head(jnp.exp(cums[rs, :]), heads, head_dim)).astype(BF16)


def intra_block(order, count, frames_in, gate_in, in_keys, out_keys, step_t, cums, skip, rows):
    width = frames_in.shape[1]
    nstate = in_keys.shape[1]
    heads = step_t.shape[0]
    return pl.pallas_call(
        intra_kernel,
        grid_spec=pltpu.PrefetchScalarGridSpec(
            num_scalar_prefetch=1,
            grid=(count,),
            in_specs=[
                pl.BlockSpec((rows, width), lambda i, o: (o[i], 0)),
                pl.BlockSpec((rows, width), lambda i, o: (o[i], 0)),
                pl.BlockSpec((rows, nstate), lambda i, o: (o[i], 0)),
                pl.BlockSpec((rows, nstate), lambda i, o: (o[i], 0)),
                pl.BlockSpec((heads, rows), lambda i, o: (0, o[i])),
                pl.BlockSpec((heads, rows), lambda i, o: (0, o[i])),
                pl.BlockSpec((1, width), lambda i, o: (0, 0)),
            ],
            out_specs=[pl.BlockSpec((1, rows, width), lambda i, o: (i, 0, 0))] * 2,
        ),
        out_shape=[
            jax.ShapeDtypeStruct((count, rows, width), F32),
            jax.ShapeDtypeStruct((count, rows, width), BF16),
        ],
        name="intra_block",
    )(order, frames_in, gate_in, in_keys, out_keys, step_t, cums, skip)


def gate_kernel(order_ref, base_ref, slope_ref, c_ref, starts_ref, before_ref, incoming_ref, *outs):
    width = base_ref.shape[2]
    heads = before_ref.shape[1]
    head_dim = width // heads
    carry = jnp.exp(before_ref[0])
    parts = []
    for h in range(heads):
        rs = slice(h * head_dim, (h + 1) * head_dim)
        parts.append(starts_ref[0, rs, :].astype(F32) + incoming_ref[rs, :] * carry[h : h + 1, :])
    start = jnp.concatenate(parts, axis=0).astype(BF16)
    inter = dot_nt(c_ref[...], start)
    gated = (base_ref[0] + inter * slope_ref[0].astype(F32)).astype(BF16)
    for k, out_ref in enumerate(outs):

        @pl.when(pl.program_id(0) == k)
        def _():
            out_ref[...] = gated


def gated_blocks(order, base, slope, out_keys, starts, before, incoming):
    count, rows, width = base.shape
    nstate = out_keys.shape[1]
    heads = before.shape[1]
    return pl.pallas_call(
        gate_kernel,
        grid_spec=pltpu.PrefetchScalarGridSpec(
            num_scalar_prefetch=1,
            grid=(count,),
            in_specs=[
                pl.BlockSpec((1, rows, width), lambda i, o: (i, 0, 0)),
                pl.BlockSpec((1, rows, width), lambda i, o: (i, 0, 0)),
                pl.BlockSpec((rows, nstate), lambda i, o: (o[i], 0)),
                pl.BlockSpec((1, width, nstate), lambda i, o: (o[i], 0, 0)),
                pl.BlockSpec((1, heads, nstate), lambda i, o: (o[i], 0, 0)),
                pl.BlockSpec((width, nstate), lambda i, o: (0, 0)),
            ],
            out_specs=[pl.BlockSpec((rows, width), lambda i, o: (0, 0))] * count,
        ),
        out_shape=[jax.ShapeDtypeStruct((rows, width), BF16)] * count,
        name="gated_blocks",
    )(order, base, slope, out_keys, starts, before, incoming)


def project_kernel(core_ref, *refs, count):
    gs = refs[:count]
    firsts = refs[count : 2 * count]
    seconds = refs[2 * count : 3 * count]
    out_ref = refs[-1]
    half = firsts[0].shape[0]
    mine = pl.multiple_of(core_ref[0] * half, half)
    other = pl.multiple_of((1 - core_ref[0]) * half, half)
    acc = None
    for g, a, b in zip(gs, firsts, seconds):
        part = jnp.dot(g[:, pl.ds(mine, half)], a[...], preferred_element_type=F32)
        part = part + jnp.dot(g[:, pl.ds(other, half)], b[...], preferred_element_type=F32)
        acc = part if acc is None else acc + part
    out_ref[...] = acc.astype(out_ref.dtype)


def project(core, gs, firsts, seconds, dtype):
    count = len(gs)
    rows, width = gs[0].shape
    half, cols = firsts[0].shape
    tile = min(cols, 512)
    in_specs = [pl.BlockSpec((rows, width), lambda j, c: (0, 0))] * count
    in_specs += [pl.BlockSpec((half, tile), lambda j, c: (0, j))] * (2 * count)
    return pl.pallas_call(
        functools.partial(project_kernel, count=count),
        grid_spec=pltpu.PrefetchScalarGridSpec(
            num_scalar_prefetch=1,
            grid=(cols // tile,),
            in_specs=in_specs,
            out_specs=pl.BlockSpec((rows, tile), lambda j, c: (0, j)),
        ),
        out_shape=jax.ShapeDtypeStruct((rows, cols), dtype),
        name="project",
    )(core, *gs, *firsts, *seconds)


def send_kernel(chan_ref, pos_ref, near_ref, across_ref, latent_ref, *outs):
    slots, dim = outs[0].shape
    groups, rows = pos_ref.shape
    latent = (near_ref[...] + across_ref[...].astype(F32)).astype(BF16)
    latent_ref[...] = latent
    slot = lax.broadcasted_iota(jnp.int32, (slots, rows), 0)
    for k, out_ref in enumerate(outs):
        here = slot + (chan_ref[0] ^ k) * slots
        acc = None
        for g in range(groups):
            pick = jnp.where(here == pos_ref[g : g + 1, :], 1.0, 0.0).astype(BF16)
            part = jnp.dot(pick, latent[:, g * dim : (g + 1) * dim], preferred_element_type=F32)
            acc = part if acc is None else acc + part
        out_ref[...] = acc.astype(BF16)


def sent_rows(chan, pos, near, across, count, slots, dim):
    rows, cols = near.shape
    return pl.pallas_call(
        send_kernel,
        grid_spec=pltpu.PrefetchScalarGridSpec(
            num_scalar_prefetch=1,
            grid=(1,),
            in_specs=[
                pl.BlockSpec(pos.shape, lambda i, c: (0, 0)),
                pl.BlockSpec(near.shape, lambda i, c: (0, 0)),
                pl.BlockSpec(across.shape, lambda i, c: (0, 0)),
            ],
            out_specs=[pl.BlockSpec((rows, cols), lambda i, c: (0, 0))]
            + [pl.BlockSpec((slots, dim), lambda i, c: (0, 0))] * count,
        ),
        out_shape=[jax.ShapeDtypeStruct((rows, cols), BF16)]
        + [jax.ShapeDtypeStruct((slots, dim), BF16)] * count,
        name="sent_rows",
    )(chan, pos, near, across)


def norm_of(v):
    return jnp.sqrt(jnp.sum(v * v, axis=-1, keepdims=True) + 1e-06)


def grad_kernel(pos_ref, latent_ref, up_ref, q_ref, out_ref):
    entries, dim = q_ref.shape
    rows = latent_ref.shape[0]
    groups = latent_ref.shape[1] // dim
    slot = lax.broadcasted_iota(jnp.int32, (rows, entries), 1)
    for n in range(groups):
        cols = slice(n * dim, (n + 1) * dim)
        pick = jnp.where(slot == pos_ref[:, n : n + 1], 1.0, 0.0).astype(BF16)
        q = jnp.dot(pick, q_ref[...], preferred_element_type=F32)
        e = latent_ref[:, cols].astype(F32)
        g = up_ref[:, cols].astype(F32)
        ne = norm_of(e)
        nq = norm_of(q)
        eh = e / ne
        qh = q / nq
        summed = eh + qh
        unit = summed / norm_of(summed)
        along = jnp.sum(unit * g, axis=-1, keepdims=True)
        toward = jnp.sum(qh * g, axis=-1, keepdims=True)
        out_ref[:, cols] = (nq / ne) * (g - 2.0 * unit * along + 2.0 * eh * toward) + (
            2.0 * COMMIT
        ) * (e - q)


def latent_grads(pos_cols, latent, upstream, q):
    rows, width = latent.shape
    groups = pos_cols.shape[1]
    tile = min(rows, 128)
    return pl.pallas_call(
        grad_kernel,
        grid=(rows // tile,),
        in_specs=[
            pl.BlockSpec((tile, groups), lambda i: (i, 0)),
            pl.BlockSpec((tile, width), lambda i: (i, 0)),
            pl.BlockSpec((tile, width), lambda i: (i, 0)),
            pl.BlockSpec(q.shape, lambda i: (0, 0)),
        ],
        out_specs=pl.BlockSpec((tile, width), lambda i: (i, 0)),
        out_shape=jax.ShapeDtypeStruct((rows, width), F32),
        name="latent_grads",
    )(pos_cols, latent, upstream, q)


def order_kernel(chan_ref, place_ref, picked_ref, *refs):
    chunks = refs[:-1]
    out_ref = refs[-1]
    tile = out_ref.shape[0]
    slots = chunks[0].shape[0]
    joined = max(1, min(len(chunks), 256 // slots))
    slot = lax.broadcasted_iota(jnp.int32, (tile, joined * slots), 0) + pl.program_id(0) * tile
    acc = None
    for n in range(0, len(chunks), joined):
        here = []
        values = []
        for k in range(n, n + joined):
            source = chan_ref[0] ^ k
            here.append(place_ref[source])
            q = picked_ref[source].astype(F32)
            values.append((q - chunks[k][...].astype(F32)).astype(BF16))
        pick = jnp.where(slot == jnp.concatenate(here, axis=1), 1.0, 0.0).astype(BF16)
        part = jnp.dot(pick, jnp.concatenate(values, axis=0), preferred_element_type=F32)
        acc = part if acc is None else acc + part
    out_ref[...] = acc.astype(BF16)


def ordered(chan, place, picked, chunks):
    slots, dim = chunks[0].shape
    total = slots * len(chunks)
    tile = min(total, 512)
    return pl.pallas_call(
        order_kernel,
        grid_spec=pltpu.PrefetchScalarGridSpec(
            num_scalar_prefetch=1,
            grid=(total // tile,),
            in_specs=[
                pl.BlockSpec(place.shape, lambda i, c: (0, 0, 0)),
                pl.BlockSpec(picked.shape, lambda i, c: (0, 0, 0)),
            ]
            + [pl.BlockSpec((slots, dim), lambda i, c: (0, 0))] * len(chunks),
            out_specs=pl.BlockSpec((tile, dim), lambda i, c: (i, 0)),
        ),
        out_shape=jax.ShapeDtypeStruct((total, dim), BF16),
        name="ordered",
    )(chan, place, picked, *chunks)


def table_kernel(bounds_ref, codes_ref, *refs, window, codes):
    runs = refs[:-1]
    out_ref = refs[-1]
    length = runs[0].shape[0]
    parts = out_ref.shape[0] // codes

    def gathered(part, turn):
        block = pl.program_id(0) * parts + part
        code = lax.broadcasted_iota(jnp.int32, (codes, window * len(runs)), 0) + block * codes
        picks = []
        rows = []
        for r, run in enumerate(runs):
            first = (bounds_ref[r, block] // 16) * 16 + turn * window
            at = pl.multiple_of(jnp.minimum(first, length - window), 16)
            lane = pl.multiple_of((at // 128) * 128, 128)
            near = codes_ref[r : r + 1, pl.ds(lane, 256)]
            near = pltpu.roll(jnp.broadcast_to(near, (8, 256)), (lane - at) % 256, 1)
            near = near[0:1, :window]
            col = lax.broadcasted_iota(jnp.int32, (1, window), 1) + at
            picks.append(jnp.where(col >= first, near, -1))
            rows.append(run[pl.ds(at, window), :])
        pick = jnp.where(jnp.concatenate(picks, axis=1) == code, 2.0, 0.0).astype(BF16)
        return jnp.dot(pick, jnp.concatenate(rows, axis=0), preferred_element_type=F32)

    for part in range(parts):
        out_ref[part * codes : (part + 1) * codes, :] = gathered(part, 0)
    for part in range(parts):
        block = pl.program_id(0) * parts + part
        turns = 0
        for r in range(len(runs)):
            lo = (bounds_ref[r, block] // 16) * 16
            turns = jnp.maximum(turns, (bounds_ref[r, block + 1] - lo + window - 1) // window)

        def more(turn, carry):
            out_ref[part * codes : (part + 1) * codes, :] += gathered(part, turn)
            return carry

        lax.fori_loop(1, turns, more, 0)


def table(bounds, codes, runs, codes_dev):
    length, dim = runs[0].shape
    block = min(CODE_BLOCK, codes_dev)
    blocks = codes_dev // block
    parts = 4
    while blocks % parts:
        parts //= 2
    window = 16
    while window < 128 and window < length and window < 2 * length // blocks:
        window *= 2
    return pl.pallas_call(
        functools.partial(table_kernel, window=window, codes=block),
        grid_spec=pltpu.PrefetchScalarGridSpec(
            num_scalar_prefetch=1,
            grid=(blocks // parts,),
            in_specs=[pl.BlockSpec(codes.shape, lambda i, b: (0, 0))]
            + [pl.BlockSpec((length, dim), lambda i, b: (0, 0))] * len(runs),
            out_specs=pl.BlockSpec((parts * block, dim), lambda i, b: (i, 0)),
        ),
        out_shape=jax.ShapeDtypeStruct((codes_dev, dim), F32),
        name="table",
    )(bounds, codes, *runs)


def layer(
    frames_in,
    gate_in,
    in_keys,
    out_keys,
    step_size,
    decay_rate,
    skip_gain,
    out_weight,
    codebook,
    code_index,
    upstream,
):
    chans = lax.axis_size("chan")
    seqs = lax.axis_size("seq")
    chan = lax.axis_index("chan").astype(jnp.int32)
    seq = lax.axis_index("seq").astype(jnp.int32)
    half = chans // 2
    core = seq % 2
    frames, width = frames_in.shape
    rows = frames // chans
    codes_dev, dim = codebook.shape
    groups = code_index.shape[1]
    heads = decay_rate.shape[0]
    head_dim = width // heads

    entries = rows * groups
    slots = max(1, (entries + chans - 1) // chans)
    flat = code_index.T.reshape(entries)
    owner = flat // codes_dev
    within = flat - owner * codes_dev
    hot = (owner[:, None] == jnp.arange(chans, dtype=jnp.int32)[None, :]).astype(BF16)
    entry = jnp.arange(entries, dtype=jnp.int32)
    earlier = (entry[:, None] > entry[None, :]).astype(BF16)
    counts = jnp.dot(earlier, hot, preferred_element_type=F32)
    rank = jnp.sum(counts * hot.astype(F32), axis=1).astype(jnp.int32)
    slot_of = owner * slots + rank
    pos = slot_of.reshape(groups, rows)
    wanted = jnp.sum(
        jnp.where(slot_of[None, :] == entry[:, None], within[None, :] + 1, 0), axis=1
    )
    wanted = jnp.where(wanted == 0, codes_dev, wanted - 1).reshape(chans, slots)
    wrows = out_weight.shape[0] // 2
    mine = lax.dynamic_slice_in_dim(out_weight, core * wrows, wrows, 0)
    other = lax.dynamic_slice_in_dim(out_weight, (1 - core) * wrows, wrows, 0)
    firsts = [mine] + [flip(mine, "chan", k) for k in range(1, half)]
    seconds = [other] + [flip(firsts[k], "seq", 1) for k in range(1, half)]

    step_t = step_size.T
    rate = decay_rate.reshape(heads, 1)
    starts, cums, before, held, sent = block_states(frames_in, in_keys, step_t, rate, rows)
    held_log = -jnp.sum(step_t * rate, axis=1)
    lower_log = jnp.zeros_like(held_log)

    def rows_of(logs, use, otherwise):
        return jnp.repeat(jnp.where(use, jnp.exp(logs), otherwise), head_dim)[:, None]

    factors = []
    bit = 1
    while bit < seqs:
        got_log = flip(held_log, "seq", bit)
        after = (seq & bit) != 0
        factors.append(
            (
                rows_of(lower_log, after, 0.0),
                rows_of(held_log, after, 1.0),
                rows_of(got_log, ~after, 1.0),
            )
        )
        lower_log = jnp.where(after, lower_log + got_log, lower_log)
        held_log = held_log + got_log
        bit *= 2
    incoming = jnp.zeros_like(held)
    bit = 1
    for to_incoming, to_got, to_held in factors:
        got = flip(sent, "seq", bit).astype(F32)
        incoming = incoming + to_incoming * got
        held = to_got * got + to_held * held
        sent = held.astype(BF16)
        bit *= 2

    top = chan // half
    low = chan % half
    turn = jnp.arange(half, dtype=jnp.int32)
    near = jnp.concatenate([top * half + (low ^ turn), core[None]])
    far = jnp.concatenate([(1 - top) * half + (low ^ turn), core[None]])
    skip = jnp.repeat(skip_gain, head_dim)[None, :]

    def gated_for(which):
        base, slope = intra_block(
            which, half, frames_in, gate_in, in_keys, out_keys, step_t, cums, skip, rows
        )
        return gated_blocks(which, base, slope, out_keys, starts, before, incoming)

    def exchanged(out):
        return [out[0]] + [flip(out[k], "chan", k) for k in range(1, half)]

    far_out = gated_for(far)
    far_blocks = exchanged(far_out)
    near, _ = lax.optimization_barrier((near, far_out))
    near_out = gated_for(near)
    near_blocks = exchanged(near_out)
    wanted, _ = lax.optimization_barrier((wanted, near_out))
    received = lax.all_to_all(wanted, "chan", split_axis=0, concat_axis=0, tiled=True)
    far_sums = project(core[None], far_blocks, firsts, seconds, BF16)
    across = flip(far_sums, "chan", half)
    near_sums = project(core[None], near_blocks, firsts, seconds, F32)

    asked = received.reshape(1, entries)
    bit = seqs // 2
    while bit > 1:
        asked = jnp.concatenate([asked, flip(asked, "seq", bit)])
        bit //= 2
    picked = jnp.take(
        codebook, jnp.minimum(asked, codes_dev - 1).reshape(-1, slots), axis=0
    ).reshape(-1, chans, slots, dim)
    keys = asked * entries + entry[None, :]
    ranks = jnp.sum((keys[:, None, :] < keys[:, :, None]).astype(jnp.int32), axis=2)
    run_codes = jnp.sum(
        jnp.where(ranks[:, None, :] == entry[None, :, None], asked[:, None, :], 0), axis=2
    )
    if seqs > 1:
        run_codes = jnp.concatenate([run_codes, flip(run_codes, "seq", 1)])
    block = min(CODE_BLOCK, codes_dev)
    edges = jnp.arange(codes_dev // block + 1, dtype=jnp.int32) * block
    bounds = jnp.sum((run_codes[:, None, :] < edges[None, :, None]).astype(jnp.int32), axis=2)
    run_codes = jnp.pad(run_codes, ((0, 0), (0, 256)), constant_values=-1)

    near_sums, ranks, run_codes, bounds, picked = lax.optimization_barrier(
        (near_sums, ranks, run_codes, bounds, picked)
    )
    latent, *sends = sent_rows(chan[None], pos, near_sums, across, chans, slots, dim)
    arrived = {0: sends[0]}
    for k in range(1, chans):
        arrived[k] = flip(sends[k], "chan", k)
    back, _ = lax.optimization_barrier((picked[0], sends[0]))
    q = lax.all_to_all(back, "chan", split_axis=0, concat_axis=0, tiled=True)
    chunks = []
    for k in range(chans):
        got = [arrived[k]]
        bit = seqs // 2
        while bit > 1:
            got = got + [flip(a, "seq", bit) for a in got]
            bit //= 2
        chunks.append(got)
    runs = [
        ordered(
            chan[None],
            ranks[r].reshape(chans, 1, slots),
            picked[r],
            [chunks[k][r] for k in range(chans)],
        )
        for r in range(max(1, seqs // 2))
    ]
    if seqs > 1:
        runs = runs + [flip(a, "seq", 1) for a in runs]
    codebook_grad = table(bounds, run_codes, runs, codes_dev)
    latent_grad = latent_grads(pos.T, latent, upstream, q.reshape(entries, dim))
    return (latent, latent_grad, codebook_grad)


def solution(mesh):
    placed = (
        P("seq", "chan"),
        P("seq", "chan"),
        P("seq", None),
        P("seq", None),
        P("seq", "chan"),
        P("chan"),
        P("chan"),
        P("chan", None),
        P("chan", None),
        P(("seq", "chan"), None),
        P(("seq", "chan"), None),
    )
    return jax.shard_map(
        layer,
        mesh=mesh,
        in_specs=placed,
        out_specs=(P(("seq", "chan"), None), P(("seq", "chan"), None), P("chan", None)),
        check_vma=False,
    )
```

```python
import functools

import jax
import jax.numpy as jnp
from jax import lax
from jax.experimental import pallas as pl
from jax.experimental.pallas import tpu as pltpu
from jax.sharding import PartitionSpec as P


COMMIT = 0.25
CODE_BLOCK = 256
TERM_ROWS = 16
GRANT = 16 * 1024 * 1024
F32 = jnp.float32
BF16 = jnp.bfloat16


def flip(x, axis, bit):
    n = lax.axis_size(axis)
    return lax.ppermute(x, axis, [(i, i ^ bit) for i in range(n)])


def dot_nt(a, b):
    return lax.dot_general(a, b, (((1,), (1,)), ((), ())), preferred_element_type=F32)


def per_head(values, heads, width):
    rows = values.shape[0]
    return jnp.concatenate(
        [jnp.broadcast_to(values[:, h : h + 1], (rows, width)) for h in range(heads)], axis=1
    )


def three_terms(value):
    one = value.astype(BF16).astype(F32)
    two = (value - one).astype(BF16).astype(F32)
    return one, two, value - one - two


def states_kernel(
    x_ref, b_ref, dt_ref, rate_ref, starts_ref, cums_ref, before_ref, sent_ref,
    state, seen, upper,
):
    step = pl.program_id(0)
    rows, width = x_ref.shape
    heads = dt_ref.shape[0]
    head_dim = width // heads

    @pl.when(step == 0)
    def _():
        state[...] = jnp.zeros_like(state)
        seen[...] = jnp.zeros_like(seen)
        upper[...] = jnp.where(
            lax.broadcasted_iota(jnp.int32, (rows, rows), 0)
            <= lax.broadcasted_iota(jnp.int32, (rows, rows), 1),
            1.0,
            0.0,
        ).astype(BF16)

    dt = dt_ref[...]
    same = lax.broadcasted_iota(jnp.int32, (heads, heads), 0) == lax.broadcasted_iota(
        jnp.int32, (heads, heads), 1
    )
    rate = jnp.sum(jnp.where(same, rate_ref[...], 0.0), axis=1, keepdims=True)
    logs = -dt * rate
    one, two, three = three_terms(logs)
    terms = jnp.concatenate([one, two, three, jnp.zeros_like(one)], axis=0).astype(BF16)
    sums = jnp.dot(terms, upper[...], preferred_element_type=F32)
    cums = sums[:heads] + sums[heads : 2 * heads] + sums[2 * heads : 3 * heads]
    cums_ref[...] = cums
    before_ref[0] = seen[...]
    total = cums[:, rows - 1 : rows]
    weight = dt * jnp.exp(total - cums)
    x_t = x_ref[...].T
    scaled = jnp.concatenate(
        [
            (x_t[h * head_dim : (h + 1) * head_dim, :].astype(F32) * weight[h : h + 1, :]).astype(
                BF16
            )
            for h in range(heads)
        ],
        axis=0,
    )
    fresh = jnp.dot(scaled, b_ref[...], preferred_element_type=F32)
    starts_ref[0] = state[...].astype(BF16)
    keep = jnp.exp(jnp.broadcast_to(total, seen.shape))
    for h in range(heads):
        rs = slice(h * head_dim, (h + 1) * head_dim)
        state[rs, :] = state[rs, :] * keep[h : h + 1, :] + fresh[rs, :]
    seen[...] = seen[...] + total

    @pl.when(step == pl.num_programs(0) - 1)
    def _():
        sent_ref[:width, :] = state[...].astype(BF16)
        for n, term in enumerate(three_terms(seen[...])):
            at = width + n * TERM_ROWS
            fill = jnp.zeros((TERM_ROWS - heads, term.shape[1]), F32)
            sent_ref[at : at + TERM_ROWS, :] = jnp.concatenate([term, fill], axis=0).astype(BF16)


def block_states(frames_in, in_keys, step_t, rate, rows):
    frames, width = frames_in.shape
    nstate = in_keys.shape[1]
    heads = step_t.shape[0]
    nb = frames // rows
    return pl.pallas_call(
        states_kernel,
        grid=(nb,),
        in_specs=[
            pl.BlockSpec((rows, width), lambda i: (i, 0)),
            pl.BlockSpec((rows, nstate), lambda i: (i, 0)),
            pl.BlockSpec((heads, rows), lambda i: (0, i)),
            pl.BlockSpec((1, heads), lambda i: (0, 0)),
        ],
        out_specs=[
            pl.BlockSpec((1, width, nstate), lambda i: (i, 0, 0)),
            pl.BlockSpec((heads, rows), lambda i: (0, i)),
            pl.BlockSpec((1, heads, nstate), lambda i: (i, 0, 0)),
            pl.BlockSpec((width + 3 * TERM_ROWS, nstate), lambda i: (0, 0)),
        ],
        out_shape=[
            jax.ShapeDtypeStruct((nb, width, nstate), BF16),
            jax.ShapeDtypeStruct((heads, frames), F32),
            jax.ShapeDtypeStruct((nb, heads, nstate), F32),
            jax.ShapeDtypeStruct((width + 3 * TERM_ROWS, nstate), BF16),
        ],
        scratch_shapes=[
            pltpu.VMEM((width, nstate), F32),
            pltpu.VMEM((heads, nstate), F32),
            pltpu.VMEM((rows, rows), BF16),
        ],
        name="block_states",
        compiler_params=pltpu.CompilerParams(vmem_limit_bytes=GRANT),
    )(frames_in, in_keys, step_t, rate)


def intra_kernel(
    order_ref, x_ref, gate_ref, b_ref, c_ref, dt_ref, cums_ref, skip_ref, base_ref, slope_ref
):
    rows, width = x_ref.shape
    heads = dt_ref.shape[0]
    head_dim = width // heads
    tile = min(rows, 128)
    cums_t = cums_ref[...]
    cums = cums_t.T
    dt = dt_ref[...]
    skip = per_head(skip_ref[...], heads, head_dim)
    for t in range(rows // tile):
        rs = slice(t * tile, (t + 1) * tile)
        n = (t + 1) * tile
        gram = dot_nt(c_ref[rs, :], b_ref[0:n, :])
        allowed = (
            lax.broadcasted_iota(jnp.int32, (tile, n), 0) + t * tile
            >= lax.broadcasted_iota(jnp.int32, (tile, n), 1)
        )
        parts = []
        for h in range(heads):
            spread = cums[rs, h : h + 1] - cums_t[h : h + 1, 0:n]
            mask = jnp.exp(jnp.where(allowed, spread, -1e30)) * dt[h : h + 1, 0:n]
            parts.append(
                jnp.dot(
                    (mask * gram).astype(BF16),
                    x_ref[0:n, h * head_dim : (h + 1) * head_dim],
                    preferred_element_type=F32,
                )
            )
        gate = gate_ref[rs, :].astype(F32)
        gate = gate / (1.0 + jnp.exp(-gate))
        mixed = jnp.concatenate(parts, axis=1) + x_ref[rs, :].astype(F32) * skip
        base_ref[0, rs, :] = mixed * gate
        slope_ref[0, rs, :] = (gate * per_head(jnp.exp(cums[rs, :]), heads, head_dim)).astype(BF16)


def intra_block(order, count, frames_in, gate_in, in_keys, out_keys, step_t, cums, skip, rows):
    width = frames_in.shape[1]
    nstate = in_keys.shape[1]
    heads = step_t.shape[0]
    return pl.pallas_call(
        intra_kernel,
        grid_spec=pltpu.PrefetchScalarGridSpec(
            num_scalar_prefetch=1,
            grid=(count,),
            in_specs=[
                pl.BlockSpec((rows, width), lambda i, o: (o[0] ^ i, 0)),
                pl.BlockSpec((rows, width), lambda i, o: (o[0] ^ i, 0)),
                pl.BlockSpec((rows, nstate), lambda i, o: (o[0] ^ i, 0)),
                pl.BlockSpec((rows, nstate), lambda i, o: (o[0] ^ i, 0)),
                pl.BlockSpec((heads, rows), lambda i, o: (0, o[0] ^ i)),
                pl.BlockSpec((heads, rows), lambda i, o: (0, o[0] ^ i)),
                pl.BlockSpec((1, heads), lambda i, o: (0, 0)),
            ],
            out_specs=[pl.BlockSpec((1, rows, width), lambda i, o: (i, 0, 0))] * 2,
        ),
        out_shape=[
            jax.ShapeDtypeStruct((count, rows, width), F32),
            jax.ShapeDtypeStruct((count, rows, width), BF16),
        ],
        name="intra_block",
        compiler_params=pltpu.CompilerParams(vmem_limit_bytes=GRANT),
    )(order, frames_in, gate_in, in_keys, out_keys, step_t, cums, skip)


def gate_kernel(
    order_ref, base_ref, slope_ref, c_ref, starts_ref, before_ref, *refs, peers
):
    states = refs[:peers]
    outs = refs[peers:-1]
    incoming = refs[-1]
    width = base_ref.shape[2]
    heads = before_ref.shape[1]
    head_dim = width // heads
    runs = [slice(h * head_dim, (h + 1) * head_dim) for h in range(heads)]

    @pl.when(pl.program_id(0) == 0)
    def _():
        seq = order_ref[1]
        logs = [
            sum(
                s[width + n * TERM_ROWS : width + (n + 1) * TERM_ROWS, :].astype(F32)
                for n in range(3)
            )
            for s in states
        ]
        factors = []
        for j in range(1, peers + 1):
            log = jnp.zeros_like(logs[0])
            for i in range(1, peers + 1):
                between = ((seq ^ j) < (seq ^ i)) & ((seq ^ i) < seq)
                log = log + jnp.where(between, logs[i - 1], 0.0)
            factors.append(jnp.where((seq ^ j) < seq, jnp.exp(log), 0.0))
        for h, rs in enumerate(runs):
            total = jnp.zeros((head_dim, incoming.shape[1]), F32)
            for factor, state in zip(factors, states):
                total = total + factor[h : h + 1, :] * state[rs, :].astype(F32)
            incoming[rs, :] = total

    carry = jnp.exp(before_ref[0])
    parts = [
        starts_ref[0, rs, :].astype(F32) + incoming[rs, :] * carry[h : h + 1, :]
        for h, rs in enumerate(runs)
    ]
    start = jnp.concatenate(parts, axis=0).astype(BF16)
    inter = dot_nt(c_ref[...], start)
    gated = (base_ref[0] + inter * slope_ref[0].astype(F32)).astype(BF16)
    for k, out_ref in enumerate(outs):

        @pl.when(pl.program_id(0) == k)
        def _():
            out_ref[...] = gated


def gated_blocks(order, base, slope, out_keys, starts, before, states):
    count, rows, width = base.shape
    nstate = out_keys.shape[1]
    heads = before.shape[1]
    return pl.pallas_call(
        functools.partial(gate_kernel, peers=len(states)),
        grid_spec=pltpu.PrefetchScalarGridSpec(
            num_scalar_prefetch=1,
            grid=(count,),
            in_specs=[
                pl.BlockSpec((1, rows, width), lambda i, o: (i, 0, 0)),
                pl.BlockSpec((1, rows, width), lambda i, o: (i, 0, 0)),
                pl.BlockSpec((rows, nstate), lambda i, o: (o[0] ^ i, 0)),
                pl.BlockSpec((1, width, nstate), lambda i, o: (o[0] ^ i, 0, 0)),
                pl.BlockSpec((1, heads, nstate), lambda i, o: (o[0] ^ i, 0, 0)),
            ]
            + [pl.BlockSpec(s.shape, lambda i, o: (0, 0)) for s in states],
            out_specs=[pl.BlockSpec((rows, width), lambda i, o: (0, 0))] * count,
            scratch_shapes=[pltpu.VMEM((width, nstate), F32)],
        ),
        out_shape=[jax.ShapeDtypeStruct((rows, width), BF16)] * count,
        name="gated_blocks",
        compiler_params=pltpu.CompilerParams(vmem_limit_bytes=GRANT),
    )(order, base, slope, out_keys, starts, before, *states)


def project_kernel(place_ref, *refs, count, shares):
    gs = refs[:count]
    ws = list(refs[count : count + 2 * sum(shares)])
    outs = refs[count + 2 * sum(shares) :]
    half = gs[0].shape[1] // 2
    acc = None
    for side in range(2):
        start = (place_ref[0] ^ side) * half
        for g, share in zip(gs, shares):
            pieces = [ws.pop(0) for _ in range(share)]
            width = half // share
            values = [
                g[:, pl.ds(pl.multiple_of(start + (place_ref[1] * (share - 1) ^ n) * width, width), width)]
                for n in range(share)
            ]
            part = jnp.dot(
                values[0] if share == 1 else jnp.concatenate(values, axis=1),
                pieces[0][...]
                if share == 1
                else jnp.concatenate([piece[...] for piece in pieces], axis=0),
                preferred_element_type=F32,
            )
            acc = part if acc is None else acc + part
    if len(outs) == 1:
        outs[0][...] = acc.astype(outs[0].dtype)
    else:
        per = pl.num_programs(0) // len(outs)
        for n, out_ref in enumerate(outs):

            @pl.when(pl.program_id(0) // per == n)
            def _():
                out_ref[...] = acc.astype(out_ref.dtype)


def project(place, gs, weight, firsts, seconds, dtype, pieces):
    count = len(gs)
    rows, width = gs[0].shape
    half, cols = width // 2, weight.shape[1]
    tile = min(cols // pieces, 512)
    per = cols // tile // pieces

    def piece(n):
        return pl.BlockSpec((rows, tile), lambda j, c: (0, jnp.clip(j - n * per, 0, per - 1)))

    def specs(parts):
        return [pl.BlockSpec((w.shape[0], tile), lambda j, c: (0, j)) for ws in parts for w in ws]

    in_specs = [pl.BlockSpec((rows, width), lambda j, c: (0, 0))] * count
    in_specs += [pl.BlockSpec((half, tile), lambda j, c: (c[0], j))] + specs(firsts)
    in_specs += [pl.BlockSpec((half, tile), lambda j, c: (1 - c[0], j))] + specs(seconds)
    return pl.pallas_call(
        functools.partial(
            project_kernel, count=count, shares=[1] + [len(ws) for ws in firsts]
        ),
        grid_spec=pltpu.PrefetchScalarGridSpec(
            num_scalar_prefetch=1,
            grid=(cols // tile,),
            in_specs=in_specs,
            out_specs=[piece(n) for n in range(pieces)],
        ),
        out_shape=[jax.ShapeDtypeStruct((rows, cols // pieces), dtype)] * pieces,
        name="project",
        compiler_params=pltpu.CompilerParams(vmem_limit_bytes=GRANT),
    )(
        place,
        *gs,
        weight,
        *[w for ws in firsts for w in ws],
        weight,
        *[w for ws in seconds for w in ws],
    )


def send_kernel(chan_ref, pos_ref, near_ref, across_ref, later_ref, latent_ref, *outs):
    slots, dim = outs[0].shape
    groups, rows = pos_ref.shape
    across = jnp.concatenate([across_ref[...], later_ref[...]], axis=1).astype(F32)
    latent = (near_ref[...] + across).astype(BF16)
    latent_ref[...] = latent
    slot = lax.broadcasted_iota(jnp.int32, (slots, rows), 0)
    for k, out_ref in enumerate(outs):
        here = slot + (chan_ref[0] ^ k) * slots
        acc = None
        for g in range(groups):
            pick = jnp.where(here == pos_ref[g : g + 1, :], 1.0, 0.0).astype(BF16)
            part = jnp.dot(pick, latent[:, g * dim : (g + 1) * dim], preferred_element_type=F32)
            acc = part if acc is None else acc + part
        out_ref[...] = acc.astype(BF16)


def sent_rows(chan, pos, near, across, count, slots, dim):
    rows, cols = near.shape
    return pl.pallas_call(
        send_kernel,
        grid_spec=pltpu.PrefetchScalarGridSpec(
            num_scalar_prefetch=1,
            grid=(1,),
            in_specs=[
                pl.BlockSpec(pos.shape, lambda i, c: (0, 0)),
                pl.BlockSpec(near.shape, lambda i, c: (0, 0)),
                pl.BlockSpec(across[0].shape, lambda i, c: (0, 0)),
                pl.BlockSpec(across[1].shape, lambda i, c: (0, 0)),
            ],
            out_specs=[pl.BlockSpec((rows, cols), lambda i, c: (0, 0))]
            + [pl.BlockSpec((slots, dim), lambda i, c: (0, 0))] * count,
        ),
        out_shape=[jax.ShapeDtypeStruct((rows, cols), BF16)]
        + [jax.ShapeDtypeStruct((slots, dim), BF16)] * count,
        name="sent_rows",
        compiler_params=pltpu.CompilerParams(vmem_limit_bytes=GRANT),
    )(chan, pos, near, *across)


def norm_of(v):
    return jnp.sqrt(jnp.sum(v * v, axis=-1, keepdims=True) + 1e-06)


def grad_kernel(pos_ref, latent_ref, up_ref, q_ref, out_ref):
    entries, dim = q_ref.shape
    rows = latent_ref.shape[0]
    groups = latent_ref.shape[1] // dim
    slot = lax.broadcasted_iota(jnp.int32, (rows, entries), 1)
    for n in range(groups):
        cols = slice(n * dim, (n + 1) * dim)
        pick = jnp.where(slot == pos_ref[:, n : n + 1], 1.0, 0.0).astype(BF16)
        q = jnp.dot(pick, q_ref[...], preferred_element_type=F32)
        e = latent_ref[:, cols].astype(F32)
        g = up_ref[:, cols].astype(F32)
        ne = norm_of(e)
        nq = norm_of(q)
        eh = e / ne
        qh = q / nq
        summed = eh + qh
        unit = summed / norm_of(summed)
        along = jnp.sum(unit * g, axis=-1, keepdims=True)
        toward = jnp.sum(qh * g, axis=-1, keepdims=True)
        out_ref[:, cols] = (nq / ne) * (g - 2.0 * unit * along + 2.0 * eh * toward) + (
            2.0 * COMMIT
        ) * (e - q)


def latent_grads(pos_cols, latent, upstream, q):
    rows, width = latent.shape
    groups = pos_cols.shape[1]
    tile = min(rows, 128)
    return pl.pallas_call(
        grad_kernel,
        grid=(rows // tile,),
        in_specs=[
            pl.BlockSpec((tile, groups), lambda i: (i, 0)),
            pl.BlockSpec((tile, width), lambda i: (i, 0)),
            pl.BlockSpec((tile, width), lambda i: (i, 0)),
            pl.BlockSpec(q.shape, lambda i: (0, 0)),
        ],
        out_specs=pl.BlockSpec((tile, width), lambda i: (i, 0)),
        out_shape=jax.ShapeDtypeStruct((rows, width), F32),
        name="latent_grads",
        compiler_params=pltpu.CompilerParams(vmem_limit_bytes=GRANT),
    )(pos_cols, latent, upstream, q)


def order_kernel(chan_ref, place_ref, picked_ref, *refs):
    chunks = refs[:-1]
    out_ref = refs[-1]
    tile = out_ref.shape[0]
    slots = chunks[0].shape[0]
    joined = max(1, min(len(chunks), 256 // slots))
    slot = lax.broadcasted_iota(jnp.int32, (tile, joined * slots), 0) + pl.program_id(0) * tile
    acc = None
    for n in range(0, len(chunks), joined):
        here = []
        values = []
        for k in range(n, n + joined):
            source = chan_ref[0] ^ k
            here.append(place_ref[source])
            q = picked_ref[source].astype(F32)
            values.append((q - chunks[k][...].astype(F32)).astype(BF16))
        pick = jnp.where(slot == jnp.concatenate(here, axis=1), 1.0, 0.0).astype(BF16)
        part = jnp.dot(pick, jnp.concatenate(values, axis=0), preferred_element_type=F32)
        acc = part if acc is None else acc + part
    out_ref[...] = acc.astype(BF16)


def ordered(chan, place, picked, chunks):
    slots, dim = chunks[0].shape
    total = slots * len(chunks)
    tile = min(total, 512)
    return pl.pallas_call(
        order_kernel,
        grid_spec=pltpu.PrefetchScalarGridSpec(
            num_scalar_prefetch=1,
            grid=(total // tile,),
            in_specs=[
                pl.BlockSpec(place.shape, lambda i, c: (0, 0, 0)),
                pl.BlockSpec(picked.shape, lambda i, c: (0, 0, 0)),
            ]
            + [pl.BlockSpec((slots, dim), lambda i, c: (0, 0))] * len(chunks),
            out_specs=pl.BlockSpec((tile, dim), lambda i, c: (i, 0)),
        ),
        out_shape=jax.ShapeDtypeStruct((total, dim), BF16),
        name="ordered",
        compiler_params=pltpu.CompilerParams(vmem_limit_bytes=GRANT),
    )(chan, place, picked, *chunks)


def table_kernel(bounds_ref, codes_ref, *refs, window, codes):
    runs = refs[:-1]
    out_ref = refs[-1]
    length = runs[0].shape[0]
    parts = out_ref.shape[0] // codes

    def gathered(part, turn):
        block = pl.program_id(0) * parts + part
        code = lax.broadcasted_iota(jnp.int32, (codes, window * len(runs)), 0) + block * codes
        picks = []
        rows = []
        for r, run in enumerate(runs):
            first = (bounds_ref[r, block] // 16) * 16 + turn * window
            at = pl.multiple_of(jnp.minimum(first, length - window), 16)
            lane = pl.multiple_of((at // 128) * 128, 128)
            near = codes_ref[r : r + 1, pl.ds(lane, 256)]
            near = pltpu.roll(jnp.broadcast_to(near, (8, 256)), (lane - at) % 256, 1)
            near = near[0:1, :window]
            col = lax.broadcasted_iota(jnp.int32, (1, window), 1) + at
            picks.append(jnp.where(col >= first, near, -1))
            rows.append(run[pl.ds(at, window), :])
        pick = jnp.where(jnp.concatenate(picks, axis=1) == code, 2.0, 0.0).astype(BF16)
        return jnp.dot(pick, jnp.concatenate(rows, axis=0), preferred_element_type=F32)

    for part in range(parts):
        out_ref[part * codes : (part + 1) * codes, :] = gathered(part, 0)
    for part in range(parts):
        block = pl.program_id(0) * parts + part
        turns = 0
        for r in range(len(runs)):
            lo = (bounds_ref[r, block] // 16) * 16
            turns = jnp.maximum(turns, (bounds_ref[r, block + 1] - lo + window - 1) // window)

        def more(turn, carry):
            out_ref[part * codes : (part + 1) * codes, :] += gathered(part, turn)
            return carry

        lax.fori_loop(1, turns, more, 0)


def table(bounds, codes, runs, codes_dev):
    length, dim = runs[0].shape
    block = min(CODE_BLOCK, codes_dev)
    blocks = codes_dev // block
    parts = 4
    while blocks % parts:
        parts //= 2
    window = 16
    while window < 128 and window < length and window < 2 * length // blocks:
        window *= 2
    return pl.pallas_call(
        functools.partial(table_kernel, window=window, codes=block),
        grid_spec=pltpu.PrefetchScalarGridSpec(
            num_scalar_prefetch=1,
            grid=(blocks // parts,),
            in_specs=[pl.BlockSpec(codes.shape, lambda i, b: (0, 0))]
            + [pl.BlockSpec((length, dim), lambda i, b: (0, 0))] * len(runs),
            out_specs=pl.BlockSpec((parts * block, dim), lambda i, b: (i, 0)),
        ),
        out_shape=jax.ShapeDtypeStruct((codes_dev, dim), F32),
        name="table",
        compiler_params=pltpu.CompilerParams(vmem_limit_bytes=GRANT),
    )(bounds, codes, *runs)


def layer(
    frames_in,
    gate_in,
    in_keys,
    out_keys,
    step_size,
    decay_rate,
    skip_gain,
    out_weight,
    codebook,
    code_index,
    upstream,
):
    chans = lax.axis_size("chan")
    seqs = lax.axis_size("seq")
    chan = lax.axis_index("chan").astype(jnp.int32)
    seq = lax.axis_index("seq").astype(jnp.int32)
    half = chans // 2
    core = seq % 2
    frames, _ = frames_in.shape
    rows = frames // chans
    codes_dev, dim = codebook.shape
    groups = code_index.shape[1]
    heads = decay_rate.shape[0]

    wrows = out_weight.shape[0] // 2
    share = (seq // 2) % 2
    split = seqs >= 4 and wrows % 256 == 0
    mine = lax.dynamic_slice_in_dim(out_weight, core * wrows, wrows, 0)
    firsts = [None] * half
    for k in sorted(range(1, half), key=lambda k: (k & (k - 1) == 0, k)):
        if k & (k - 1) and split:
            part = lax.dynamic_slice_in_dim(
                out_weight, core * wrows + share * (wrows // 2), wrows // 2, 0
            )
            part = flip(part, "chan", k)
            firsts[k] = [part, flip(part, "seq", 2)]
        else:
            firsts[k] = [flip(mine, "chan", k)]
    firsts = firsts[1:]
    seconds = [[flip(w, "seq", 1) for w in ws] for ws in firsts]

    step_t = step_size.T
    starts, cums, before, sent = block_states(
        frames_in, in_keys, step_t, decay_rate.reshape(1, heads), rows
    )
    states = {k: flip(sent, "seq", k) for k in list(range(2, seqs)) + [1]}
    states = [states[k] for k in range(1, seqs)]
    skip = skip_gain.reshape(1, heads)

    def gated_for(which):
        base, slope = intra_block(
            which, half, frames_in, gate_in, in_keys, out_keys, step_t, cums, skip, rows
        )
        return gated_blocks(which, base, slope, out_keys, starts, before, states)

    def exchanged(out):
        return [out[0]] + [flip(out[k], "chan", k) for k in range(1, half)]

    far_out = gated_for(jnp.stack([chan ^ half, seq]))
    far_blocks = exchanged(far_out)
    near, _ = lax.optimization_barrier((jnp.stack([chan, seq]), far_out))
    near_out = gated_for(near)
    near_blocks = exchanged(near_out)
    entries = rows * groups
    slots = max(1, (entries + chans - 1) // chans)
    flat = code_index.T.reshape(entries)
    owner = flat // codes_dev
    within = flat - owner * codes_dev
    hot = (owner[:, None] == jnp.arange(chans, dtype=jnp.int32)[None, :]).astype(BF16)
    entry = jnp.arange(entries, dtype=jnp.int32)
    earlier = (entry[:, None] > entry[None, :]).astype(BF16)
    counts = jnp.dot(earlier, hot, preferred_element_type=F32)
    rank = jnp.sum(counts * hot.astype(F32), axis=1).astype(jnp.int32)
    slot_of = owner * slots + rank
    pos = slot_of.reshape(groups, rows)
    wanted = jnp.sum(
        jnp.where(slot_of[None, :] == entry[:, None], within[None, :] + 1, 0), axis=1
    )
    wanted = jnp.where(wanted == 0, codes_dev, wanted - 1).reshape(chans, slots)
    received = lax.all_to_all(wanted, "chan", split_axis=0, concat_axis=0, tiled=True)

    far_sums = project(jnp.stack([core, share]), far_blocks, out_weight, firsts, seconds, BF16, 2)
    across = [flip(far_sums[0], "chan", half)]
    across.append(flip(far_sums[1], "chan", half))
    (near_sums,) = project(jnp.stack([core, share]), near_blocks, out_weight, firsts, seconds, F32, 1)

    asked = received.reshape(1, entries)
    bit = seqs // 2
    while bit > 1:
        asked = jnp.concatenate([asked, flip(asked, "seq", bit)])
        bit //= 2
    picked = jnp.take(
        codebook, jnp.minimum(asked, codes_dev - 1).reshape(-1, slots), axis=0
    ).reshape(-1, chans, slots, dim)
    keys = asked * entries + entry[None, :]
    ranks = jnp.sum((keys[:, None, :] < keys[:, :, None]).astype(jnp.int32), axis=2)
    run_codes = jnp.sum(
        jnp.where(ranks[:, None, :] == entry[None, :, None], asked[:, None, :], 0), axis=2
    )
    if seqs > 1:
        run_codes = jnp.concatenate([run_codes, flip(run_codes, "seq", 1)])
    block = min(CODE_BLOCK, codes_dev)
    edges = jnp.arange(codes_dev // block + 1, dtype=jnp.int32) * block
    bounds = jnp.sum((run_codes[:, None, :] < edges[None, :, None]).astype(jnp.int32), axis=2)
    run_codes = jnp.pad(run_codes, ((0, 0), (0, 256)), constant_values=-1)

    near_sums, ranks, run_codes, bounds, picked, back = lax.optimization_barrier(
        (near_sums, ranks, run_codes, bounds, picked, picked[0])
    )
    latent, *sends = sent_rows(chan[None], pos, near_sums, across, chans, slots, dim)
    arrived = {0: sends[0]}
    for k in range(1, chans):
        arrived[k] = flip(sends[k], "chan", k)
    back, _ = lax.optimization_barrier((back, sends[0]))
    q = lax.all_to_all(back, "chan", split_axis=0, concat_axis=0, tiled=True)
    chunks = []
    for k in range(chans):
        got = [arrived[k]]
        bit = seqs // 2
        while bit > 1:
            got = got + [flip(a, "seq", bit) for a in got]
            bit //= 2
        chunks.append(got)
    runs = [
        ordered(
            chan[None],
            ranks[r].reshape(chans, 1, slots),
            picked[r],
            [chunks[k][r] for k in range(chans)],
        )
        for r in range(max(1, seqs // 2))
    ]
    if seqs > 1:
        runs = runs + [flip(a, "seq", 1) for a in runs]
    codebook_grad = table(bounds, run_codes, runs, codes_dev)
    latent_grad = latent_grads(pos.T, latent, upstream, q.reshape(entries, dim))
    return (latent, latent_grad, codebook_grad)


def solution(mesh):
    placed = (
        P("seq", "chan"),
        P("seq", "chan"),
        P("seq", None),
        P("seq", None),
        P("seq", "chan"),
        P("chan"),
        P("chan"),
        P("chan", None),
        P("chan", None),
        P(("seq", "chan"), None),
        P(("seq", "chan"), None),
    )
    return jax.shard_map(
        layer,
        mesh=mesh,
        in_specs=placed,
        out_specs=(P(("seq", "chan"), None), P(("seq", "chan"), None), P("chan", None)),
        check_vma=False,
    )
```

```python
import functools

import jax
import jax.numpy as jnp
from jax import lax
from jax.experimental import pallas as pl
from jax.experimental.pallas import tpu as pltpu
from jax.sharding import PartitionSpec as P


COMMIT = 0.25
CODE_BLOCK = 256
TERM_ROWS = 16
GRANT = 16 * 1024 * 1024
F32 = jnp.float32
BF16 = jnp.bfloat16


def flip(x, axis, bit):
    n = lax.axis_size(axis)
    return lax.ppermute(x, axis, [(i, i ^ bit) for i in range(n)])


def dot_nt(a, b):
    return lax.dot_general(a, b, (((1,), (1,)), ((), ())), preferred_element_type=F32)


def per_head(values, heads, width):
    rows = values.shape[0]
    return jnp.concatenate(
        [jnp.broadcast_to(values[:, h : h + 1], (rows, width)) for h in range(heads)], axis=1
    )


def three_terms(value):
    one = value.astype(BF16).astype(F32)
    two = (value - one).astype(BF16).astype(F32)
    return one, two, value - one - two


def states_kernel(
    x_ref, b_ref, dt_ref, rate_ref, starts_ref, cums_ref, before_ref, sent_ref,
    state, seen, upper,
):
    step = pl.program_id(0)
    rows, width = x_ref.shape
    heads = dt_ref.shape[0]
    head_dim = width // heads

    @pl.when(step == 0)
    def _():
        state[...] = jnp.zeros_like(state)
        seen[...] = jnp.zeros_like(seen)
        upper[...] = jnp.where(
            lax.broadcasted_iota(jnp.int32, (rows, rows), 0)
            <= lax.broadcasted_iota(jnp.int32, (rows, rows), 1),
            1.0,
            0.0,
        ).astype(BF16)

    dt = dt_ref[...]
    same = lax.broadcasted_iota(jnp.int32, (heads, heads), 0) == lax.broadcasted_iota(
        jnp.int32, (heads, heads), 1
    )
    rate = jnp.sum(jnp.where(same, rate_ref[...], 0.0), axis=1, keepdims=True)
    logs = -dt * rate
    one, two, three = three_terms(logs)
    terms = jnp.concatenate([one, two, three, jnp.zeros_like(one)], axis=0).astype(BF16)
    sums = jnp.dot(terms, upper[...], preferred_element_type=F32)
    cums = sums[:heads] + sums[heads : 2 * heads] + sums[2 * heads : 3 * heads]
    cums_ref[...] = cums
    before_ref[0] = seen[...]
    total = cums[:, rows - 1 : rows]
    weight = dt * jnp.exp(total - cums)
    x_t = x_ref[...].T
    scaled = jnp.concatenate(
        [
            (x_t[h * head_dim : (h + 1) * head_dim, :].astype(F32) * weight[h : h + 1, :]).astype(
                BF16
            )
            for h in range(heads)
        ],
        axis=0,
    )
    fresh = jnp.dot(scaled, b_ref[...], preferred_element_type=F32)
    starts_ref[0] = state[...].astype(BF16)
    keep = jnp.exp(jnp.broadcast_to(total, seen.shape))
    for h in range(heads):
        rs = slice(h * head_dim, (h + 1) * head_dim)
        state[rs, :] = state[rs, :] * keep[h : h + 1, :] + fresh[rs, :]
    seen[...] = seen[...] + total

    @pl.when(step == pl.num_programs(0) - 1)
    def _():
        sent_ref[:width, :] = state[...].astype(BF16)
        for n, term in enumerate(three_terms(seen[...])):
            at = width + n * TERM_ROWS
            fill = jnp.zeros((TERM_ROWS - heads, term.shape[1]), F32)
            sent_ref[at : at + TERM_ROWS, :] = jnp.concatenate([term, fill], axis=0).astype(BF16)


def block_states(frames_in, in_keys, step_t, rate, rows):
    frames, width = frames_in.shape
    nstate = in_keys.shape[1]
    heads = step_t.shape[0]
    nb = frames // rows
    return pl.pallas_call(
        states_kernel,
        grid=(nb,),
        in_specs=[
            pl.BlockSpec((rows, width), lambda i: (i, 0)),
            pl.BlockSpec((rows, nstate), lambda i: (i, 0)),
            pl.BlockSpec((heads, rows), lambda i: (0, i)),
            pl.BlockSpec((1, heads), lambda i: (0, 0)),
        ],
        out_specs=[
            pl.BlockSpec((1, width, nstate), lambda i: (i, 0, 0)),
            pl.BlockSpec((heads, rows), lambda i: (0, i)),
            pl.BlockSpec((1, heads, nstate), lambda i: (i, 0, 0)),
            pl.BlockSpec((width + 3 * TERM_ROWS, nstate), lambda i: (0, 0)),
        ],
        out_shape=[
            jax.ShapeDtypeStruct((nb, width, nstate), BF16),
            jax.ShapeDtypeStruct((heads, frames), F32),
            jax.ShapeDtypeStruct((nb, heads, nstate), F32),
            jax.ShapeDtypeStruct((width + 3 * TERM_ROWS, nstate), BF16),
        ],
        scratch_shapes=[
            pltpu.VMEM((width, nstate), F32),
            pltpu.VMEM((heads, nstate), F32),
            pltpu.VMEM((rows, rows), BF16),
        ],
        name="block_states",
        compiler_params=pltpu.CompilerParams(vmem_limit_bytes=GRANT),
    )(frames_in, in_keys, step_t, rate)


def intra_kernel(
    order_ref, x_ref, gate_ref, b_ref, c_ref, dt_ref, cums_ref, skip_ref, base_ref, slope_ref
):
    rows, width = x_ref.shape
    heads = dt_ref.shape[0]
    head_dim = width // heads
    tile = min(rows, 128)
    cums_t = cums_ref[...]
    cums = cums_t.T
    dt = dt_ref[...]
    skip = per_head(skip_ref[...], heads, head_dim)
    for t in range(rows // tile):
        rs = slice(t * tile, (t + 1) * tile)
        n = (t + 1) * tile
        gram = dot_nt(c_ref[rs, :], b_ref[0:n, :])
        allowed = (
            lax.broadcasted_iota(jnp.int32, (tile, n), 0) + t * tile
            >= lax.broadcasted_iota(jnp.int32, (tile, n), 1)
        )
        parts = []
        for h in range(heads):
            spread = cums[rs, h : h + 1] - cums_t[h : h + 1, 0:n]
            mask = jnp.exp(jnp.where(allowed, spread, -1e30)) * dt[h : h + 1, 0:n]
            parts.append(
                jnp.dot(
                    (mask * gram).astype(BF16),
                    x_ref[0:n, h * head_dim : (h + 1) * head_dim],
                    preferred_element_type=F32,
                )
            )
        gate = gate_ref[rs, :].astype(F32)
        gate = gate / (1.0 + jnp.exp(-gate))
        mixed = jnp.concatenate(parts, axis=1) + x_ref[rs, :].astype(F32) * skip
        base_ref[0, rs, :] = mixed * gate
        slope_ref[0, rs, :] = (gate * per_head(jnp.exp(cums[rs, :]), heads, head_dim)).astype(BF16)


def intra_block(order, count, frames_in, gate_in, in_keys, out_keys, step_t, cums, skip, rows):
    width = frames_in.shape[1]
    nstate = in_keys.shape[1]
    heads = step_t.shape[0]
    return pl.pallas_call(
        intra_kernel,
        grid_spec=pltpu.PrefetchScalarGridSpec(
            num_scalar_prefetch=1,
            grid=(count,),
            in_specs=[
                pl.BlockSpec((rows, width), lambda i, o: (o[0] ^ i, 0)),
                pl.BlockSpec((rows, width), lambda i, o: (o[0] ^ i, 0)),
                pl.BlockSpec((rows, nstate), lambda i, o: (o[0] ^ i, 0)),
                pl.BlockSpec((rows, nstate), lambda i, o: (o[0] ^ i, 0)),
                pl.BlockSpec((heads, rows), lambda i, o: (0, o[0] ^ i)),
                pl.BlockSpec((heads, rows), lambda i, o: (0, o[0] ^ i)),
                pl.BlockSpec((1, heads), lambda i, o: (0, 0)),
            ],
            out_specs=[pl.BlockSpec((1, rows, width), lambda i, o: (i, 0, 0))] * 2,
        ),
        out_shape=[
            jax.ShapeDtypeStruct((count, rows, width), F32),
            jax.ShapeDtypeStruct((count, rows, width), BF16),
        ],
        name="intra_block",
        compiler_params=pltpu.CompilerParams(vmem_limit_bytes=GRANT),
    )(order, frames_in, gate_in, in_keys, out_keys, step_t, cums, skip)


def gate_kernel(
    order_ref, base_ref, slope_ref, c_ref, starts_ref, before_ref, *refs, peers
):
    states = refs[:peers]
    outs = refs[peers:-1]
    incoming = refs[-1]
    width = base_ref.shape[2]
    heads = before_ref.shape[1]
    head_dim = width // heads
    runs = [slice(h * head_dim, (h + 1) * head_dim) for h in range(heads)]

    @pl.when(pl.program_id(0) == 0)
    def _():
        seq = order_ref[1]
        logs = [
            sum(
                s[width + n * TERM_ROWS : width + (n + 1) * TERM_ROWS, :].astype(F32)
                for n in range(3)
            )
            for s in states
        ]
        factors = []
        for j in range(1, peers + 1):
            log = jnp.zeros_like(logs[0])
            for i in range(1, peers + 1):
                between = ((seq ^ j) < (seq ^ i)) & ((seq ^ i) < seq)
                log = log + jnp.where(between, logs[i - 1], 0.0)
            factors.append(jnp.where((seq ^ j) < seq, jnp.exp(log), 0.0))
        for h, rs in enumerate(runs):
            total = jnp.zeros((head_dim, incoming.shape[1]), F32)
            for factor, state in zip(factors, states):
                total = total + factor[h : h + 1, :] * state[rs, :].astype(F32)
            incoming[rs, :] = total

    carry = jnp.exp(before_ref[0])
    parts = [
        starts_ref[0, rs, :].astype(F32) + incoming[rs, :] * carry[h : h + 1, :]
        for h, rs in enumerate(runs)
    ]
    start = jnp.concatenate(parts, axis=0).astype(BF16)
    inter = dot_nt(c_ref[...], start)
    gated = (base_ref[0] + inter * slope_ref[0].astype(F32)).astype(BF16)
    for k, out_ref in enumerate(outs):

        @pl.when(pl.program_id(0) == k)
        def _():
            out_ref[...] = gated


def gated_blocks(order, base, slope, out_keys, starts, before, states):
    count, rows, width = base.shape
    nstate = out_keys.shape[1]
    heads = before.shape[1]
    return pl.pallas_call(
        functools.partial(gate_kernel, peers=len(states)),
        grid_spec=pltpu.PrefetchScalarGridSpec(
            num_scalar_prefetch=1,
            grid=(count,),
            in_specs=[
                pl.BlockSpec((1, rows, width), lambda i, o: (i, 0, 0)),
                pl.BlockSpec((1, rows, width), lambda i, o: (i, 0, 0)),
                pl.BlockSpec((rows, nstate), lambda i, o: (o[0] ^ i, 0)),
                pl.BlockSpec((1, width, nstate), lambda i, o: (o[0] ^ i, 0, 0)),
                pl.BlockSpec((1, heads, nstate), lambda i, o: (o[0] ^ i, 0, 0)),
            ]
            + [pl.BlockSpec(s.shape, lambda i, o: (0, 0)) for s in states],
            out_specs=[pl.BlockSpec((rows, width), lambda i, o: (0, 0))] * count,
            scratch_shapes=[pltpu.VMEM((width, nstate), F32)],
        ),
        out_shape=[jax.ShapeDtypeStruct((rows, width), BF16)] * count,
        name="gated_blocks",
        compiler_params=pltpu.CompilerParams(vmem_limit_bytes=GRANT),
    )(order, base, slope, out_keys, starts, before, *states)


def project_kernel(place_ref, *refs, count, shares):
    gs = refs[:count]
    ws = list(refs[count : count + 2 * sum(shares)])
    outs = refs[count + 2 * sum(shares) :]
    half = gs[0].shape[1] // 2
    acc = None
    for side in range(2):
        start = (place_ref[0] ^ side) * half
        for g, share in zip(gs, shares):
            pieces = [ws.pop(0) for _ in range(share)]
            width = half // share
            values = [
                g[:, pl.ds(pl.multiple_of(start + (place_ref[1] * (share - 1) ^ n) * width, width), width)]
                for n in range(share)
            ]
            part = jnp.dot(
                values[0] if share == 1 else jnp.concatenate(values, axis=1),
                pieces[0][...]
                if share == 1
                else jnp.concatenate([piece[...] for piece in pieces], axis=0),
                preferred_element_type=F32,
            )
            acc = part if acc is None else acc + part
    if len(outs) == 1:
        outs[0][...] = acc.astype(outs[0].dtype)
    else:
        per = pl.num_programs(0) // len(outs)
        for n, out_ref in enumerate(outs):

            @pl.when(pl.program_id(0) // per == n)
            def _():
                out_ref[...] = acc.astype(out_ref.dtype)


def project(place, gs, weight, firsts, seconds, dtype, pieces):
    count = len(gs)
    rows, width = gs[0].shape
    half, cols = width // 2, weight.shape[1]
    tile = min(cols // pieces, 512)
    per = cols // tile // pieces

    def piece(n):
        return pl.BlockSpec((rows, tile), lambda j, c: (0, jnp.clip(j - n * per, 0, per - 1)))

    def specs(parts):
        return [pl.BlockSpec((w.shape[0], tile), lambda j, c: (0, j)) for ws in parts for w in ws]

    in_specs = [pl.BlockSpec((rows, width), lambda j, c: (0, 0))] * count
    in_specs += [pl.BlockSpec((half, tile), lambda j, c: (c[0], j))] + specs(firsts)
    in_specs += [pl.BlockSpec((half, tile), lambda j, c: (1 - c[0], j))] + specs(seconds)
    return pl.pallas_call(
        functools.partial(
            project_kernel, count=count, shares=[1] + [len(ws) for ws in firsts]
        ),
        grid_spec=pltpu.PrefetchScalarGridSpec(
            num_scalar_prefetch=1,
            grid=(cols // tile,),
            in_specs=in_specs,
            out_specs=[piece(n) for n in range(pieces)],
        ),
        out_shape=[jax.ShapeDtypeStruct((rows, cols // pieces), dtype)] * pieces,
        name="project",
        compiler_params=pltpu.CompilerParams(vmem_limit_bytes=GRANT),
    )(
        place,
        *gs,
        weight,
        *[w for ws in firsts for w in ws],
        weight,
        *[w for ws in seconds for w in ws],
    )


def send_kernel(chan_ref, pos_ref, near_ref, across_ref, later_ref, latent_ref, *outs):
    slots, dim = outs[0].shape
    groups, rows = pos_ref.shape
    across = jnp.concatenate([across_ref[...], later_ref[...]], axis=1).astype(F32)
    latent = (near_ref[...] + across).astype(BF16)
    latent_ref[...] = latent
    slot = lax.broadcasted_iota(jnp.int32, (slots, rows), 0)
    for k, out_ref in enumerate(outs):
        here = slot + (chan_ref[0] ^ k) * slots
        acc = None
        for g in range(groups):
            pick = jnp.where(here == pos_ref[g : g + 1, :], 1.0, 0.0).astype(BF16)
            part = jnp.dot(pick, latent[:, g * dim : (g + 1) * dim], preferred_element_type=F32)
            acc = part if acc is None else acc + part
        out_ref[...] = acc.astype(BF16)


def sent_rows(chan, pos, near, across, count, slots, dim):
    rows, cols = near.shape
    return pl.pallas_call(
        send_kernel,
        grid_spec=pltpu.PrefetchScalarGridSpec(
            num_scalar_prefetch=1,
            grid=(1,),
            in_specs=[
                pl.BlockSpec(pos.shape, lambda i, c: (0, 0)),
                pl.BlockSpec(near.shape, lambda i, c: (0, 0)),
                pl.BlockSpec(across[0].shape, lambda i, c: (0, 0)),
                pl.BlockSpec(across[1].shape, lambda i, c: (0, 0)),
            ],
            out_specs=[pl.BlockSpec((rows, cols), lambda i, c: (0, 0))]
            + [pl.BlockSpec((slots, dim), lambda i, c: (0, 0))] * count,
        ),
        out_shape=[jax.ShapeDtypeStruct((rows, cols), BF16)]
        + [jax.ShapeDtypeStruct((slots, dim), BF16)] * count,
        name="sent_rows",
        compiler_params=pltpu.CompilerParams(vmem_limit_bytes=GRANT),
    )(chan, pos, near, *across)


def norm_of(v):
    return jnp.sqrt(jnp.sum(v * v, axis=-1, keepdims=True) + 1e-06)


def grad_kernel(pos_ref, latent_ref, up_ref, q_ref, out_ref):
    entries, dim = q_ref.shape
    rows = latent_ref.shape[0]
    groups = latent_ref.shape[1] // dim
    slot = lax.broadcasted_iota(jnp.int32, (rows, entries), 1)
    for n in range(groups):
        cols = slice(n * dim, (n + 1) * dim)
        pick = jnp.where(slot == pos_ref[:, n : n + 1], 1.0, 0.0).astype(BF16)
        q = jnp.dot(pick, q_ref[...], preferred_element_type=F32)
        e = latent_ref[:, cols].astype(F32)
        g = up_ref[:, cols].astype(F32)
        ne = norm_of(e)
        nq = norm_of(q)
        eh = e / ne
        qh = q / nq
        summed = eh + qh
        unit = summed / norm_of(summed)
        along = jnp.sum(unit * g, axis=-1, keepdims=True)
        toward = jnp.sum(qh * g, axis=-1, keepdims=True)
        out_ref[:, cols] = (nq / ne) * (g - 2.0 * unit * along + 2.0 * eh * toward) + (
            2.0 * COMMIT
        ) * (e - q)


def latent_grads(pos_cols, latent, upstream, q):
    rows, width = latent.shape
    groups = pos_cols.shape[1]
    latent, upstream = [
        pltpu.with_memory_space_constraint(x, pltpu.HBM) for x in (latent, upstream)
    ]
    tile = min(rows, 128)
    return pl.pallas_call(
        grad_kernel,
        grid=(rows // tile,),
        in_specs=[
            pl.BlockSpec((tile, groups), lambda i: (i, 0)),
            pl.BlockSpec((tile, width), lambda i: (i, 0)),
            pl.BlockSpec((tile, width), lambda i: (i, 0)),
            pl.BlockSpec(q.shape, lambda i: (0, 0)),
        ],
        out_specs=pl.BlockSpec((tile, width), lambda i: (i, 0)),
        out_shape=jax.ShapeDtypeStruct((rows, width), F32),
        name="latent_grads",
        compiler_params=pltpu.CompilerParams(vmem_limit_bytes=GRANT),
    )(pos_cols, latent, upstream, q)


def order_kernel(chan_ref, place_ref, picked_ref, *refs):
    chunks = refs[:-1]
    out_ref = refs[-1]
    tile = out_ref.shape[0]
    slots = chunks[0].shape[0]
    joined = max(1, min(len(chunks), 256 // slots))
    slot = lax.broadcasted_iota(jnp.int32, (tile, joined * slots), 0) + pl.program_id(0) * tile
    acc = None
    for n in range(0, len(chunks), joined):
        here = []
        values = []
        for k in range(n, n + joined):
            source = chan_ref[0] ^ k
            here.append(place_ref[source])
            q = picked_ref[source].astype(F32)
            values.append((q - chunks[k][...].astype(F32)).astype(BF16))
        pick = jnp.where(slot == jnp.concatenate(here, axis=1), 1.0, 0.0).astype(BF16)
        part = jnp.dot(pick, jnp.concatenate(values, axis=0), preferred_element_type=F32)
        acc = part if acc is None else acc + part
    out_ref[...] = acc.astype(BF16)


def ordered(chan, place, picked, chunks):
    slots, dim = chunks[0].shape
    total = slots * len(chunks)
    tile = min(total, 512)
    return pl.pallas_call(
        order_kernel,
        grid_spec=pltpu.PrefetchScalarGridSpec(
            num_scalar_prefetch=1,
            grid=(total // tile,),
            in_specs=[
                pl.BlockSpec(place.shape, lambda i, c: (0, 0, 0)),
                pl.BlockSpec(picked.shape, lambda i, c: (0, 0, 0)),
            ]
            + [pl.BlockSpec((slots, dim), lambda i, c: (0, 0))] * len(chunks),
            out_specs=pl.BlockSpec((tile, dim), lambda i, c: (i, 0)),
        ),
        out_shape=jax.ShapeDtypeStruct((total, dim), BF16),
        name="ordered",
        compiler_params=pltpu.CompilerParams(vmem_limit_bytes=GRANT),
    )(chan, place, picked, *chunks)


def table_kernel(bounds_ref, codes_ref, *refs, window, codes):
    runs = refs[:-1]
    out_ref = refs[-1]
    length = runs[0].shape[0]
    parts = out_ref.shape[0] // codes

    def gathered(part, turn):
        block = pl.program_id(0) * parts + part
        code = lax.broadcasted_iota(jnp.int32, (codes, window * len(runs)), 0) + block * codes
        picks = []
        rows = []
        for r, run in enumerate(runs):
            first = (bounds_ref[r, block] // 16) * 16 + turn * window
            at = pl.multiple_of(jnp.minimum(first, length - window), 16)
            lane = pl.multiple_of((at // 128) * 128, 128)
            near = codes_ref[r : r + 1, pl.ds(lane, 256)]
            near = pltpu.roll(jnp.broadcast_to(near, (8, 256)), (lane - at) % 256, 1)
            near = near[0:1, :window]
            col = lax.broadcasted_iota(jnp.int32, (1, window), 1) + at
            picks.append(jnp.where(col >= first, near, -1))
            rows.append(run[pl.ds(at, window), :])
        pick = jnp.where(jnp.concatenate(picks, axis=1) == code, 2.0, 0.0).astype(BF16)
        return jnp.dot(pick, jnp.concatenate(rows, axis=0), preferred_element_type=F32)

    for part in range(parts):
        out_ref[part * codes : (part + 1) * codes, :] = gathered(part, 0)
    for part in range(parts):
        block = pl.program_id(0) * parts + part
        turns = 0
        for r in range(len(runs)):
            lo = (bounds_ref[r, block] // 16) * 16
            turns = jnp.maximum(turns, (bounds_ref[r, block + 1] - lo + window - 1) // window)

        def more(turn, carry):
            out_ref[part * codes : (part + 1) * codes, :] += gathered(part, turn)
            return carry

        lax.fori_loop(1, turns, more, 0)


def table(bounds, codes, runs, codes_dev):
    length, dim = runs[0].shape
    block = min(CODE_BLOCK, codes_dev)
    blocks = codes_dev // block
    parts = 4
    while blocks % parts:
        parts //= 2
    window = 16
    while window < 128 and window < length and window < 2 * length // blocks:
        window *= 2
    return pl.pallas_call(
        functools.partial(table_kernel, window=window, codes=block),
        grid_spec=pltpu.PrefetchScalarGridSpec(
            num_scalar_prefetch=1,
            grid=(blocks // parts,),
            in_specs=[pl.BlockSpec(codes.shape, lambda i, b: (0, 0))]
            + [pl.BlockSpec((length, dim), lambda i, b: (0, 0))] * len(runs),
            out_specs=pl.BlockSpec((parts * block, dim), lambda i, b: (i, 0)),
        ),
        out_shape=jax.ShapeDtypeStruct((codes_dev, dim), F32),
        name="table",
        compiler_params=pltpu.CompilerParams(vmem_limit_bytes=GRANT),
    )(bounds, codes, *runs)


def layer(
    frames_in,
    gate_in,
    in_keys,
    out_keys,
    step_size,
    decay_rate,
    skip_gain,
    out_weight,
    codebook,
    code_index,
    upstream,
):
    chans = lax.axis_size("chan")
    seqs = lax.axis_size("seq")
    chan = lax.axis_index("chan").astype(jnp.int32)
    seq = lax.axis_index("seq").astype(jnp.int32)
    half = chans // 2
    core = seq % 2
    frames, _ = frames_in.shape
    rows = frames // chans
    codes_dev, dim = codebook.shape
    groups = code_index.shape[1]
    heads = decay_rate.shape[0]

    wrows = out_weight.shape[0] // 2
    share = (seq // 2) % 2
    split = seqs >= 4 and wrows % 256 == 0
    mine = lax.dynamic_slice_in_dim(out_weight, core * wrows, wrows, 0)
    firsts = [None] * half
    for k in sorted(range(1, half), key=lambda k: (k & (k - 1) == 0, k)):
        if k & (k - 1) and split:
            part = lax.dynamic_slice_in_dim(
                out_weight, core * wrows + share * (wrows // 2), wrows // 2, 0
            )
            part = flip(part, "chan", k)
            firsts[k] = [part, flip(part, "seq", 2)]
        else:
            firsts[k] = [flip(mine, "chan", k)]
    firsts = firsts[1:]
    seconds = [[flip(w, "seq", 1) for w in ws] for ws in firsts]

    step_t = step_size.T
    starts, cums, before, sent = block_states(
        frames_in, in_keys, step_t, decay_rate.reshape(1, heads), rows
    )
    states = {k: flip(sent, "seq", k) for k in list(range(2, seqs)) + [1]}
    states = [states[k] for k in range(1, seqs)]
    skip = skip_gain.reshape(1, heads)

    def gated_for(which):
        base, slope = intra_block(
            which, half, frames_in, gate_in, in_keys, out_keys, step_t, cums, skip, rows
        )
        return gated_blocks(which, base, slope, out_keys, starts, before, states)

    def exchanged(out):
        return [out[0]] + [flip(out[k], "chan", k) for k in range(1, half)]

    far_out = gated_for(jnp.stack([chan ^ half, seq]))
    far_blocks = exchanged(far_out)
    code_index, _ = lax.optimization_barrier((code_index, far_out))

    entries = rows * groups
    slots = max(1, (entries + chans - 1) // chans)
    flat = code_index.T.reshape(entries)
    owner = flat // codes_dev
    within = flat - owner * codes_dev
    hot = (owner[:, None] == jnp.arange(chans, dtype=jnp.int32)[None, :]).astype(BF16)
    entry = jnp.arange(entries, dtype=jnp.int32)
    earlier = (entry[:, None] > entry[None, :]).astype(BF16)
    counts = jnp.dot(earlier, hot, preferred_element_type=F32)
    rank = jnp.sum(counts * hot.astype(F32), axis=1).astype(jnp.int32)
    slot_of = owner * slots + rank
    pos = slot_of.reshape(groups, rows)
    wanted = jnp.sum(
        jnp.where(slot_of[None, :] == entry[:, None], within[None, :] + 1, 0), axis=1
    )
    wanted = jnp.where(wanted == 0, codes_dev, wanted - 1).reshape(chans, slots)
    received = lax.all_to_all(wanted, "chan", split_axis=0, concat_axis=0, tiled=True)

    far_sums = project(jnp.stack([core, share]), far_blocks, out_weight, firsts, seconds, BF16, 2)
    across = [flip(far_sums[0], "chan", half)]
    near, _ = lax.optimization_barrier((jnp.stack([chan, seq]), far_sums))
    near_out = gated_for(near)
    near_blocks = exchanged(near_out)
    across.append(flip(far_sums[1], "chan", half))
    (near_sums,) = project(jnp.stack([core, share]), near_blocks, out_weight, firsts, seconds, F32, 1)

    asked = received.reshape(1, entries)
    bit = seqs // 2
    while bit > 1:
        asked = jnp.concatenate([asked, flip(asked, "seq", bit)])
        bit //= 2
    picked = jnp.take(codebook, asked.reshape(-1, slots), axis=0, mode="clip").reshape(
        -1, chans, slots, dim
    )
    keys = asked * entries + entry[None, :]
    ranks = jnp.sum((keys[:, None, :] < keys[:, :, None]).astype(jnp.int32), axis=2)
    near_sums, asked, ranks, picked, back = lax.optimization_barrier(
        (near_sums, asked, ranks, picked, picked[0])
    )
    run_codes = jnp.sum(
        jnp.where(ranks[:, None, :] == entry[None, :, None], asked[:, None, :], 0), axis=2
    )
    if seqs > 1:
        run_codes = jnp.concatenate([run_codes, flip(run_codes, "seq", 1)])
    block = min(CODE_BLOCK, codes_dev)
    edges = jnp.arange(codes_dev // block + 1, dtype=jnp.int32) * block
    bounds = jnp.sum((run_codes[:, None, :] < edges[None, :, None]).astype(jnp.int32), axis=2)
    run_codes = jnp.pad(run_codes, ((0, 0), (0, 256)), constant_values=-1)
    latent, *sends = sent_rows(chan[None], pos, near_sums, across, chans, slots, dim)
    arrived = {0: sends[0]}
    for k in range(1, chans):
        arrived[k] = flip(sends[k], "chan", k)
    back, _ = lax.optimization_barrier((back, sends[0]))
    q = lax.all_to_all(back, "chan", split_axis=0, concat_axis=0, tiled=True)
    chunks = []
    for k in range(chans):
        got = [arrived[k]]
        bit = seqs // 2
        while bit > 1:
            got = got + [flip(a, "seq", bit) for a in got]
            bit //= 2
        chunks.append(got)
    runs = [
        ordered(
            chan[None],
            ranks[r].reshape(chans, 1, slots),
            picked[r],
            [chunks[k][r] for k in range(chans)],
        )
        for r in range(max(1, seqs // 2))
    ]
    if seqs > 1:
        runs = runs + [flip(a, "seq", 1) for a in runs]
    codebook_grad = table(bounds, run_codes, runs, codes_dev)
    latent_grad = latent_grads(pos.T, latent, upstream, q.reshape(entries, dim))
    return (latent, latent_grad, codebook_grad)


def solution(mesh):
    placed = (
        P("seq", "chan"),
        P("seq", "chan"),
        P("seq", None),
        P("seq", None),
        P("seq", "chan"),
        P("chan"),
        P("chan"),
        P("chan", None),
        P("chan", None),
        P(("seq", "chan"), None),
        P(("seq", "chan"), None),
    )
    return jax.shard_map(
        layer,
        mesh=mesh,
        in_specs=placed,
        out_specs=(P(("seq", "chan"), None), P(("seq", "chan"), None), P("chan", None)),
        check_vma=False,
    )
```
